32 devices in a mesh: groups: 2 (over x), src: 8 (over z, y), rcv: 2 (over core).
Axes of the slice: x: 2, y: 2, z: 4, core: 2. Of those that a mesh axis runs over, the one named last changes fastest.
Arguments:
- spectra: bfloat16 [1280, 2, 2, 4096], P(('groups', 'src'), None, None, 'rcv'), parts along dimension 0, may hold values from -6 to 6
- pair_bins: int32 [1280, 80], P(('groups', 'src')), parts along dimension 0, may hold values from 0 to 15
- owners: int32 [32], P('groups'), parts along dimension 0, may hold values from 0 to 15, as said below
Outputs:
- bin_stacks: float32 [64, 2, 4096], P(('groups', 'src', 'rcv')), parts along dimension 0
The draws below stay inside these ranges and needn't reach their ends.
There are 2 independent parts, one for each index of `groups`. The reference program is written for one: setup_inputs(seed, part) draws one part's arguments, and reference() takes and returns one part's arrays. A program takes and returns all parts, laid end to end along the dimension named above; each array names one. Nothing has to cross between parts.
Inputs may be any that keep to these rules, and one draw needn't show every extreme that they name: `owners`: each device owns at most 2 bins and some device owns exactly 2.
All inputs are finite; a program needn't handle non-finite values.
Results may differ from the reference program's by a relative error of at most 0.004.
Values may be sent and summed in bfloat16 or wider, within the bound.
A program may use at most 64 MiB of HBM per device.

```python
import jax
import jax.numpy as jnp
from jax import lax

CB = 80
W = 2
F = 4096
HALF = 32
CH = 640
NB = 16
ND = 16
CAP = 2
N_SRC = 8


def draw_owners(key, part):
    first_key, second_key = jax.random.split(jax.random.fold_in(key, 7))
    order = jax.random.permutation(first_key, ND * CAP)
    owner_slot = order // CAP
    leader = owner_slot[0]
    priority = jnp.where(owner_slot == leader, -1, jnp.arange(ND * CAP))
    ranked = jnp.argsort(priority, stable=True)
    chosen = owner_slot[ranked[:NB]]
    shuffle = jax.random.permutation(second_key, NB)
    return chosen[shuffle].astype(jnp.int32)


def with_ends(result, stream_key, low, high):
    longest = result.shape.index(max(result.shape))
    spots = []
    for shift in (0, 1):
        where = [jax.random.randint(jax.random.fold_in(stream_key, axis), (), 0, length) for axis, length in enumerate(result.shape)]
        where[longest] = (where[longest] + shift) % result.shape[longest]
        spots.append(tuple(where))
    return result.at[spots[0]].set(low).at[spots[1]].set(high)


def level_of(own_key, shape, pieces, smallest, high):
    loudness, own = 1.0, jax.random.fold_in(own_key, 6)
    for axis_at, blocks in pieces:
        draws = jnp.exp(jax.random.uniform(jax.random.fold_in(own, axis_at), (blocks,), jnp.float32, smallest / len(pieces), high / len(pieces)))
        loudness = loudness * jnp.repeat(draws, shape[axis_at] // blocks).reshape([-1 if axis == axis_at else 1 for axis in range(len(shape))])
    return loudness


def centred(own_key, dims, spread, reach, shards=(), kind=jnp.bfloat16):
    entries = jax.random.normal(own_key, dims, jnp.float32) * spread
    if len(shards) > 0:
        entries = level_of(own_key, dims, shards, -0.22, 0.18) * entries
    return jnp.clip(entries, min=-reach, max=reach).astype(kind)


def setup_inputs(seed: int = 0, part: int = 0) -> dict:
    seeds = jax.random.split(jax.random.key(seed), 4)
    part_splits = jax.random.split(jax.random.fold_in(seeds[3], part), 4)
    return {
        "spectra": centred(part_splits[0], (CH, W, 2, F), 1.0, 6.0, ((0, 8), (3, 2))),
        "pair_bins": with_ends(jax.random.randint(part_splits[1], (CH, CB), 0, NB), jax.random.fold_in(part_splits[1], 1), 0, NB - 1).astype(jnp.int32),
        "owners": draw_owners(jax.random.fold_in(jax.random.fold_in(seeds[3], part), 71), part),
    }


smooth_eps = 1e-06

def whiten(spectra):
    values = spectra.astype(jnp.float32)
    magnitude = jnp.sqrt(values[:, :, 0] ** 2 + values[:, :, 1] ** 2)
    padded = jnp.pad(magnitude, ((0, 0), (0, 0), (HALF, HALF)))
    total = jnp.zeros_like(magnitude)
    for offset in range(2 * HALF + 1):
        total = total + padded[:, :, offset:offset + F]
    smooth = total / (2 * HALF + 1)
    return (values / (smooth[:, :, None, :] + smooth_eps)).astype(jnp.bfloat16)

def reference(spectra, pair_bins, owners):
    white_half = whiten(spectra)
    white = lax.optimization_barrier(white_half).astype(jnp.float32)
    padded = jnp.concatenate([white, jnp.zeros((CB, W, 2, F), jnp.float32)], axis=0)
    channel_ids = jnp.arange(CH, dtype=jnp.int32)

    def per_source(carry, inputs):
        source, bins_row, channel = inputs
        block_id = channel // CB
        start = ((block_id + 1) * CB).astype(jnp.int32)
        receivers = lax.dynamic_slice_in_dim(padded, start, CB, 0)
        valid = (block_id + 1 < N_SRC).astype(jnp.float32)
        src_re = source[:, 0]
        src_im = source[:, 1]
        corr_re = lax.optimization_barrier(jnp.sum(src_re[None] * receivers[:, :, 0] + src_im[None] * receivers[:, :, 1], axis=1))
        corr_im = lax.optimization_barrier(jnp.sum(src_im[None] * receivers[:, :, 0] - src_re[None] * receivers[:, :, 1], axis=1))
        stacked = jnp.stack([corr_re, corr_im], axis=1) * valid
        stack_sum = carry[0] + jax.ops.segment_sum(stacked, bins_row, num_segments=NB)
        count_sum = carry[1] + jax.ops.segment_sum(jnp.ones((CB,), jnp.float32) * valid, bins_row, num_segments=NB)
        return ((stack_sum, count_sum), None)
    init = (jnp.zeros((NB, 2, F), jnp.float32), jnp.zeros((NB,), jnp.float32))
    (stack, counts), _ = lax.scan(per_source, init, (white, pair_bins, channel_ids))
    same = owners[:, None] == owners[None, :]
    earlier = jnp.arange(NB, dtype=jnp.int32)[None, :] < jnp.arange(NB, dtype=jnp.int32)[:, None]
    slot = lax.optimization_barrier(jnp.sum((same & earlier).astype(jnp.int32), axis=1))
    rows = (owners * CAP + slot).astype(jnp.int32)
    scaled = stack / jnp.sqrt(jnp.maximum(counts, 1.0))[:, None, None]
    return jnp.zeros((ND * CAP, 2, F), jnp.float32).at[rows].set(scaled)
```

```python
import functools

import jax
import jax.numpy as jnp
from jax import lax
from jax.experimental import pallas as pl
from jax.experimental.pallas import tpu as pltpu
from jax.sharding import PartitionSpec as P

HALF = 32
CAP = 2
LANES = 128
CHUNK = 256
smooth_eps = 1e-06
MESH = pl.DeviceIdType.MESH


def kernel(
    dims,
    x_hbm,
    lab_hbm,
    owners_hbm,
    out_ref,
    raw,
    xt,
    white,
    near,
    far,
    direct,
    mag_hi,
    mag_lo,
    edge_out,
    band,
    onehot,
    own,
    own_d,
    prod,
    acc,
    pick,
    send_part,
    recv_part,
    labels_ref,
    owners_ref,
    lab_out,
    lab_in,
    count_out,
    count_in,
    load_sems,
    near_send,
    near_recv,
    far_send,
    far_recv,
    direct_send,
    direct_recv,
    halo_send,
    halo_recv,
    lab_send,
    lab_recv,
    count_send,
    count_recv,
    part_send,
    part_recv,
):
    nsrc, nrcv, nbins, local, windows, chunks = dims
    half = chunks // 2
    relayed = half // 2
    parts = 2 * windows
    width = chunks * CHUNK
    tiles = width // LANES
    per_half = tiles // 2
    ndev = nsrc * nrcv
    s = lax.axis_index("src")
    r = lax.axis_index("rcv")
    me = s * nrcv + r
    par = lax.rem(s, 2)
    f32 = jnp.float32
    bf16 = jnp.bfloat16

    loads = [
        pltpu.make_async_copy(
            x_hbm.at[:, pl.ds(2 * per_half * h, 2 * per_half)], raw.at[h], load_sems.at[h]
        )
        for h in range(2)
    ]
    loads.append(pltpu.make_async_copy(lab_hbm, labels_ref, load_sems.at[2]))
    loads.append(pltpu.make_async_copy(owners_hbm, owners_ref, load_sems.at[3]))
    for load in loads:
        load.start()

    barrier = pltpu.get_barrier_semaphore()

    def greet(k, carry):
        o = lax.rem(me + k, ndev)
        pl.semaphore_signal(
            barrier,
            inc=1,
            device_id={"src": o // nrcv, "rcv": lax.rem(o, nrcv)},
            device_id_type=MESH,
        )
        return carry

    lax.fori_loop(1, ndev, greet, 0)

    def place(h, t):
        return h * half + r * (half - 1) + t * (1 - 2 * r)

    tall = CHUNK + 2 * LANES
    k_ids = lax.broadcasted_iota(jnp.int32, (tall, CHUNK), 0) - LANES
    n_ids = lax.broadcasted_iota(jnp.int32, (tall, CHUNK), 1)
    band[...] = jnp.where((k_ids >= n_ids - HALF) & (k_ids <= n_ids + HALF), 1.0, 0.0).astype(bf16)

    zero = jnp.zeros((windows * local, LANES), bf16)
    outer = pl.ds(pl.multiple_of(r * (LANES + width), LANES), LANES)
    for buffer in (mag_hi, mag_lo):
        buffer[:, outer] = zero

    for h in range(2):
        loads[h].wait()

    def turn_rows(c, carry):
        for w in range(windows):
            for h in range(2):
                rows = raw[h, c * windows + w].astype(f32)
                first = (w * 2 * tiles + h * 2 * per_half) * local
                xt[pl.ds(first + c, 2 * per_half, stride=local), :] = rows
        return carry

    lax.fori_loop(0, local, turn_rows, 0, unroll=4)

    def plane(w, tile, p):
        at = pl.multiple_of(((w * tiles + tile) * 2 + p) * local, 8)
        return xt[pl.ds(at, local), :]

    def magnitude(w, tile):
        re = plane(w, tile, 0)
        im = plane(w, tile, 1)
        m = jnp.sqrt(re * re + im * im)
        hi = m.astype(bf16)
        return hi, (m - hi.astype(f32)).astype(bf16)

    def magnitude_tile(tile):
        for w in range(windows):
            at = pl.ds(pl.multiple_of(LANES + tile * LANES, LANES), LANES)
            rows = pl.ds(w * local, local)
            mag_hi[rows, at], mag_lo[rows, at] = magnitude(w, tile)

    def magnitudes(j, carry):
        for d in range(CHUNK // LANES):
            magnitude_tile(j * (CHUNK // LANES) + d)
        return carry

    def inside(j):
        return jnp.minimum(jnp.maximum(j, 0), chunks - 1)

    def whiten(j):
        span = pl.ds(pl.multiple_of(j * CHUNK, LANES), tall)
        total = jnp.dot(mag_hi[:, span], band[...], preferred_element_type=f32)
        total = total + jnp.dot(mag_lo[:, span], band[...], preferred_element_type=f32)
        inverse = 1.0 / (total / (2 * HALF + 1) + smooth_eps)
        for w in range(windows):
            for d in range(CHUNK // LANES):
                lanes = slice(d * LANES, (d + 1) * LANES)
                part = inverse[w * local : (w + 1) * local, lanes]
                for p in range(2):
                    x = plane(w, j * (CHUNK // LANES) + d, p)
                    white[j, 2 * w + p, :, lanes] = (x * part).astype(bf16)

    partner = s + 1 - 2 * par
    beyond = s + 2 - 4 * par
    sends_far = (beyond >= 0) & (beyond < nsrc)
    back = s - 2 + 4 * par
    has_far = (back >= 0) & (back < nsrc)

    def near_copy(t, k):
        return pltpu.make_async_remote_copy(
            src_ref=white.at[place(1 - par, t), k],
            dst_ref=near.at[t, k],
            send_sem=near_send.at[t, k],
            recv_sem=near_recv.at[t, k],
            device_id={"src": partner},
            device_id_type=MESH,
        )

    def far_copy(t, k):
        return pltpu.make_async_remote_copy(
            src_ref=near.at[t, k],
            dst_ref=far.at[t, k],
            send_sem=far_send.at[t, k],
            recv_sem=far_recv.at[t, k],
            device_id={"src": beyond},
            device_id_type=MESH,
        )

    def direct_copy(u, k):
        return pltpu.make_async_remote_copy(
            src_ref=white.at[place(par, relayed + u), k],
            dst_ref=direct.at[u, k],
            send_sem=direct_send.at[u, k],
            recv_sem=direct_recv.at[u, k],
            device_id={"src": back},
            device_id_type=MESH,
        )


    def halo_copy(n):
        buffer = (mag_hi, mag_lo)[n]
        return pltpu.make_async_remote_copy(
            src_ref=edge_out.at[n],
            dst_ref=buffer.at[:, outer],
            send_sem=halo_send.at[n],
            recv_sem=halo_recv.at[n],
            device_id={"rcv": 1 - r},
            device_id_type=MESH,
        )

    def lab_copy(slot, to):
        return pltpu.make_async_remote_copy(
            src_ref=lab_out,
            dst_ref=lab_in.at[slot],
            send_sem=lab_send.at[slot],
            recv_sem=lab_recv.at[slot],
            device_id={"src": to},
            device_id_type=MESH,
        )

    sends_next = s + 1 < nsrc
    sends_second = (par == 1) & sends_next

    for w in range(windows):
        rows = pl.ds(w * local, local)
        edge_out[0, rows], edge_out[1, rows] = magnitude(w, (1 - r) * (tiles - 1))
    for t in range(-1, 2):
        magnitudes(inside(place(1 - par, t)), 0)
    for load in loads[2:]:
        load.wait()
    labels = labels_ref[...]
    lab_out[...] = labels.astype(f32).astype(bf16)
    whiten(place(1 - par, 0))
    pl.semaphore_wait(barrier, ndev - 1)

    def send_near(t):
        for k in range(parts):
            near_copy(t, k).start()

    send_near(0)
    for n in range(2):
        halo_copy(n).start()

    @pl.when(sends_next)
    def _():
        lab_copy(0, s + 1).start()

    @pl.when(sends_second)
    def _():
        lab_copy(1, s - 1).start()
        lab_copy(2, s + 2).start()

    def send_next(t, carry):
        magnitudes(inside(place(1 - par, t + 1)), 0)
        whiten(place(1 - par, t))
        send_near(t)
        return carry

    lax.fori_loop(1, half - 1, send_next, 0)
    magnitudes(inside(place(1 - par, half)), 0)
    for n in range(2):
        halo_copy(n).wait_recv()
    whiten(place(1 - par, half - 1))
    send_near(half - 1)

    def keep_magnitude(t, carry):
        return magnitudes(place(par, t), carry)

    lax.fori_loop(0, half, keep_magnitude, 0)

    def keep_direct(u, carry):
        whiten(place(par, relayed + u))

        @pl.when(has_far)
        def _():
            for k in range(parts):
                direct_copy(u, k).start()

        return carry

    lax.fori_loop(0, half - relayed, keep_direct, 0)

    def keep(t, carry):
        whiten(place(par, t))
        return carry

    lax.fori_loop(0, relayed, keep, 0)

    lanes = count_out.shape[1]
    lane_ids = lax.broadcasted_iota(jnp.int32, (1, lanes), 1)
    valid = sends_next.astype(f32)

    def expand(b, counted):
        hits = jnp.where(labels == b, 1.0, 0.0).astype(f32)
        onehot[0, pl.ds(pl.multiple_of(b * local, 16), local), :] = hits.astype(bf16)
        found = jnp.sum(jnp.sum(hits, axis=0, keepdims=True), axis=1, keepdims=True)
        return counted + jnp.where(lane_ids == b, found, 0.0)

    counted = lax.fori_loop(0, nbins, expand, jnp.zeros((1, lanes), f32)) * valid
    count_out[...] = counted
    count_in[s] = counted

    def count_copy(o, slot):
        return pltpu.make_async_remote_copy(
            src_ref=count_out,
            dst_ref=count_in.at[slot],
            send_sem=count_send.at[o],
            recv_sem=count_recv.at[slot],
            device_id={"src": o},
            device_id_type=MESH,
        )

    def send_count(k, carry):
        count_copy(lax.rem(s + k, nsrc), s).start()
        return carry

    lax.fori_loop(1, nsrc, send_count, 0)

    def expand_into(which, table):
        def one(b, carry):
            onehot[which, pl.ds(pl.multiple_of(b * local, 16), local), :] = jnp.where(
                table == b, 1.0, 0.0
            ).astype(bf16)
            return carry

        lax.fori_loop(0, nbins, one, 0)

    @pl.when(s > 0)
    def _():
        lab_copy(0, s).wait_recv()
        expand_into(1, jnp.transpose(lab_in[0].astype(f32)).astype(jnp.int32))

    @pl.when(sends_far & (par == 0))
    def _():
        lab_copy(1, s).wait_recv()
        expand_into(2, jnp.transpose(lab_in[1].astype(f32)).astype(jnp.int32))

    @pl.when(sends_far & (par == 1))
    def _():
        lab_copy(2, s).wait_recv()
        expand_into(2, lab_in[2].astype(f32).astype(jnp.int32))

    owned = owners_ref[...]
    b_rows = lax.broadcasted_iota(jnp.int32, (nbins, nbins), 0)
    b_cols = lax.broadcasted_iota(jnp.int32, (nbins, nbins), 1)
    column = jnp.sum(jnp.where(b_rows == b_cols, owned, 0).astype(f32), axis=1, keepdims=True)
    earlier = jnp.where((column.astype(jnp.int32) == owned) & (b_rows < b_cols), 1.0, 0.0)
    slots = jnp.sum(earlier.astype(f32), axis=0, keepdims=True)
    rows_row = (owned.astype(f32) * CAP + slots).astype(jnp.int32)
    lines = CAP * 4
    cols = 4 * nbins
    tiled = jnp.concatenate([rows_row] * 4, axis=1)
    batch = 16
    row_ids = lax.broadcasted_iota(jnp.int32, (batch * lines, cols), 0)
    col_group = lax.broadcasted_iota(jnp.int32, (batch * lines, cols), 1) // nbins
    same_line = lax.rem(row_ids, 4) == col_group
    row_slot = row_ids // 4

    def prepare(g, carry):
        chosen = same_line & (tiled == row_slot + g * (batch * CAP))
        at = pl.ds(pl.multiple_of(g * (batch * lines), 16), batch * lines)
        pick[at] = jnp.where(chosen, 1.0, 0.0).astype(bf16)
        return carry

    lax.fori_loop(0, ndev // batch, prepare, 0)

    group = min(nbins, 16)

    def correlate(which, sign, mine, other, t, k, first):
        rows = group * local
        side = lax.rem(k, 2)
        k2 = k + 1 - 2 * side
        factor = sign * (1 - 2 * side).astype(f32)

        def some(g, carry):
            picked = onehot[which, pl.ds(pl.multiple_of(g * rows, 16), rows), :]
            prod[...] = jnp.dot(picked, other[t, k], preferred_element_type=f32)
            res, ims = [], []
            for b in range(group):
                p = prod[b * local : (b + 1) * local]
                res.append(jnp.sum(mine[k] * p, axis=0, keepdims=True))
                ims.append(jnp.sum(mine[k2] * p, axis=0, keepdims=True))
            re = jnp.concatenate(res, axis=0)
            im = jnp.concatenate(ims, axis=0) * factor
            at = pl.ds(pl.multiple_of(g * group, group), group)
            for d in range(CHUNK // LANES):
                part = slice(d * LANES, (d + 1) * LANES)
                for q, value in ((0, re), (1, im)):
                    if first:
                        acc[t, 2 * d + q, at] = value[:, part]
                    else:
                        acc[t, 2 * d + q, at] += value[:, part]
            return carry

        lax.fori_loop(0, nbins // group, some, 0)

    sign_near = (1 - 2 * par).astype(f32)

    def part_copy(g, o, slot):
        return pltpu.make_async_remote_copy(
            src_ref=send_part.at[g, o],
            dst_ref=recv_part.at[g, slot],
            send_sem=part_send.at[g, o],
            recv_sem=part_recv.at[g, slot],
            device_id={"src": o // nrcv, "rcv": lax.rem(o, nrcv)},
            device_id_type=MESH,
        )

    def route(g):
        stacked = [acc[2 * g + u].reshape(cols, LANES).astype(bf16) for u in range(2)]

        def some(q, carry):
            at = pl.ds(pl.multiple_of(q * (batch * lines), 16), batch * lines)
            wide = [jnp.dot(pick[at], rhs, preferred_element_type=f32) for rhs in stacked]
            for n in range(batch):
                both = [v[n * lines : (n + 1) * lines] for v in wide]
                send_part[g, q * batch + n] = jnp.concatenate(both, axis=0).astype(bf16)
            return carry

        lax.fori_loop(0, ndev // batch, some, 0)

        def send_one(k, carry):
            part_copy(g, lax.rem(me + k, ndev), me).start()
            return carry

        lax.fori_loop(1, ndev, send_one, 0)
        recv_part[g, me] = send_part[g, me]

    def start_turn(t):
        for k in range(parts):
            own[k] = white[place(par, t), k].astype(f32)

    def relay_turn(t):
        start_turn(t)

        def piece(k, carry):
            near_copy(t, k).wait_recv()

            @pl.when(sends_far)
            def _():
                far_copy(t, k).start()

            correlate(par, sign_near, own, near, t, k, False)
            return carry

        acc[t] = jnp.zeros((4, nbins, LANES), f32)
        lax.fori_loop(0, parts, piece, 0)

    def far_turn(t):
        @pl.when(has_far)
        def _():
            start_turn(t)

            def piece(k, carry):
                far_copy(t, k).wait_recv()
                correlate(1 - par, -sign_near, own, far, t, k, False)
                return carry

            lax.fori_loop(0, parts, piece, 0)

    def direct_turn(t):
        start_turn(t)

        @pl.when(sends_far)
        def _():
            for k in range(parts):
                direct_copy(t - relayed, k).wait_recv()
                own_d[k] = direct[t - relayed, k].astype(f32)

        def piece(k, carry):
            near_copy(t, k).wait_recv()
            correlate(par, sign_near, own, near, t, k, False)

            @pl.when(sends_far)
            def _():
                correlate(2, -sign_near, own_d, near, t, k, False)

            return carry

        acc[t] = jnp.zeros((4, nbins, LANES), f32)
        lax.fori_loop(0, parts, piece, 0)

    for t in range(relayed):
        relay_turn(t)
        if t > 0:
            far_turn(t - 1)
    for t in range(relayed, half):
        direct_turn(t)
        if t == relayed:
            far_turn(relayed - 1)
            route(0)

            def take_count(k, carry):
                o = lax.rem(s + k, nsrc)
                count_copy(o, o).wait_recv()
                return carry

            lax.fori_loop(1, nsrc, take_count, 0)
    counts = jnp.sum(count_in[...], axis=0)[0:1, :nbins]
    scale = []
    for c in range(CAP):
        mine = jnp.sum(jnp.where(rows_row == me * CAP + c, counts, 0.0), axis=1, keepdims=True)
        scale.append(1.0 / jnp.sqrt(jnp.maximum(mine, 1.0)))
    route(1)

    for g in range(half // 2):

        def take_part(k, carry):
            o = lax.rem(me + k, ndev)
            part_copy(g, o, o).wait_recv()
            return carry

        lax.fori_loop(1, ndev, take_part, 0)
        for rr in range(nrcv):
            for pp in range(2):

                def add(z, total):
                    return total + recv_part[g, (2 * z + pp) * nrcv + rr].astype(f32)

                total = lax.fori_loop(0, nsrc // 2, add, jnp.zeros((2 * lines, LANES), f32))
                for u in range(2):
                    t = 2 * g + u
                    j = pp * half + rr * (half - 1) + t * (1 - 2 * rr)
                    for c in range(CAP):
                        row = (c * nrcv * chunks + rr * chunks + j) * 4
                        value = total[u * lines + c * 4 : u * lines + c * 4 + 4]
                        out_ref[row : row + 4] = value * scale[c]

    for t in range(half):
        for k in range(parts):
            near_copy(t, k).wait_send()

    @pl.when(sends_far)
    def _():
        for t in range(relayed):
            for k in range(parts):
                far_copy(t, k).wait_send()

    @pl.when(has_far)
    def _():
        for u in range(half - relayed):
            for k in range(parts):
                direct_copy(u, k).wait_send()

    for n in range(2):
        halo_copy(n).wait_send()

    @pl.when(sends_next)
    def _():
        lab_copy(0, s + 1).wait_send()

    @pl.when(sends_second)
    def _():
        lab_copy(1, s - 1).wait_send()
        lab_copy(2, s + 2).wait_send()

    def end_count(k, carry):
        count_copy(lax.rem(s + k, nsrc), s).wait_send()
        return carry

    lax.fori_loop(1, nsrc, end_count, 0)

    def end_part(k, carry):
        for g in range(half // 2):
            part_copy(g, lax.rem(me + k, ndev), me).wait_send()
        return carry

    lax.fori_loop(1, ndev, end_part, 0)


def per_device(spectra, pair_bins, owners):
    local, windows, _, width = spectra.shape
    nbins = owners.shape[0]
    nsrc = lax.axis_size("src")
    nrcv = lax.axis_size("rcv")
    ndev = nsrc * nrcv
    chunks = width // CHUNK
    half = chunks // 2
    relayed = half // 2
    tiles = width // LANES
    parts = 2 * windows
    lanes = -(-nbins // 128) * 128
    group = min(nbins, 16)
    x = spectra.reshape(local * windows, 2, tiles, LANES).transpose(0, 2, 1, 3)
    x = x.reshape(local * windows, 2 * tiles, LANES)
    dims = (nsrc, nrcv, nbins, local, windows, chunks)
    bf16, f32 = jnp.bfloat16, jnp.float32
    dma = pltpu.SemaphoreType.DMA
    hbm = pl.BlockSpec(memory_space=pltpu.HBM)
    out = pl.pallas_call(
        functools.partial(kernel, dims),
        out_shape=jax.ShapeDtypeStruct((CAP * nrcv * tiles * 2, LANES), f32),
        in_specs=[hbm] * 3,
        out_specs=pl.BlockSpec(memory_space=pltpu.VMEM),
        scratch_shapes=[
            pltpu.VMEM((2, local * windows, tiles, LANES), bf16),
            pltpu.VMEM((windows * 2 * tiles * local, LANES), f32),
            pltpu.VMEM((chunks, parts, local, CHUNK), bf16),
            pltpu.VMEM((half, parts, local, CHUNK), bf16),
            pltpu.VMEM((relayed, parts, local, CHUNK), bf16),
            pltpu.VMEM((half - relayed, parts, local, CHUNK), bf16),
            pltpu.VMEM((windows * local, width + 2 * LANES), bf16),
            pltpu.VMEM((windows * local, width + 2 * LANES), bf16),
            pltpu.VMEM((2, windows * local, LANES), bf16),
            pltpu.VMEM((CHUNK + 2 * LANES, CHUNK), bf16),
            pltpu.VMEM((3, nbins * local, local), bf16),
            pltpu.VMEM((parts, local, CHUNK), f32),
            pltpu.VMEM((parts, local, CHUNK), f32),
            pltpu.VMEM((group * local, CHUNK), f32),
            pltpu.VMEM((half, 4, nbins, LANES), f32),
            pltpu.VMEM((ndev * CAP * 4, 4 * nbins), bf16),
            pltpu.VMEM((half // 2, ndev, CAP * 8, LANES), bf16),
            pltpu.VMEM((half // 2, ndev, CAP * 8, LANES), bf16),
            pltpu.VMEM((local, local), jnp.int32),
            pltpu.VMEM((1, nbins), jnp.int32),
            pltpu.VMEM((local, local), bf16),
            pltpu.VMEM((3, local, local), bf16),
            pltpu.VMEM((1, lanes), f32),
            pltpu.VMEM((nsrc, 1, lanes), f32),
            dma((4,)),
            dma((half, parts)),
            dma((half, parts)),
            dma((relayed, parts)),
            dma((relayed, parts)),
            dma((half - relayed, parts)),
            dma((half - relayed, parts)),
            dma((2,)),
            dma((2,)),
            dma((3,)),
            dma((3,)),
            dma((nsrc,)),
            dma((nsrc,)),
            dma((half // 2, ndev)),
            dma((half // 2, ndev)),
        ],
        compiler_params=pltpu.CompilerParams(
            collective_id=0, has_side_effects=True, vmem_limit_bytes=62 * 1024 * 1024
        ),
    )(x, pair_bins, owners[None])
    out = out.reshape(CAP, nrcv * tiles, 2, LANES).transpose(0, 2, 1, 3)
    return out.reshape(CAP, 2, nrcv * width)


def solution(mesh):
    in_specs = (P(("groups", "src"), None, None, "rcv"), P(("groups", "src"), None), P("groups"))
    out_specs = P(("groups", "src", "rcv"), None, None)
    return jax.shard_map(
        per_device, mesh=mesh, in_specs=in_specs, out_specs=out_specs, check_vma=False
    )
```

```python
import functools

import jax
import jax.numpy as jnp
from jax import lax
from jax.experimental import pallas as pl
from jax.experimental.pallas import tpu as pltpu
from jax.sharding import PartitionSpec as P

HALF = 32
CAP = 2
LANES = 128
CHUNK = 256
smooth_eps = 1e-06
MESH = pl.DeviceIdType.MESH


def kernel(
    dims,
    x_hbm,
    lab_hbm,
    owners_hbm,
    out_ref,
    raw,
    xt,
    white,
    near,
    far,
    direct,
    mag_hi,
    mag_lo,
    edge_out,
    band,
    onehot,
    own,
    own_d,
    prod,
    acc,
    pick,
    send_part,
    recv_part,
    labels_ref,
    owners_ref,
    lab_out,
    lab_in,
    count_out,
    count_in,
    load_sems,
    near_send,
    near_recv,
    far_send,
    far_recv,
    direct_send,
    direct_recv,
    halo_send,
    halo_recv,
    lab_send,
    lab_recv,
    count_send,
    count_recv,
    part_send,
    part_recv,
):
    nsrc, nrcv, nbins, local, windows, chunks = dims
    half = chunks // 2
    relayed = half // 2
    parts = 2 * windows
    width = chunks * CHUNK
    tiles = width // LANES
    per_half = tiles // 2
    ndev = nsrc * nrcv
    s = lax.axis_index("src")
    r = lax.axis_index("rcv")
    me = s * nrcv + r
    par = lax.rem(s, 2)
    f32 = jnp.float32
    bf16 = jnp.bfloat16

    def load_half(n, h):
        rows = pl.ds(pl.multiple_of(h * 2 * per_half, 16), 2 * per_half)
        return pltpu.make_async_copy(x_hbm.at[:, rows], raw.at[n], load_sems.at[n])

    load_sent = load_half(0, 1 - par)
    load_kept = load_half(1, par)
    load_labels = pltpu.make_async_copy(lab_hbm, labels_ref, load_sems.at[2])
    load_owners = pltpu.make_async_copy(owners_hbm, owners_ref, load_sems.at[3])
    for load in (load_sent, load_labels, load_kept, load_owners):
        load.start()

    barrier = pltpu.get_barrier_semaphore()

    def greet(k, carry):
        o = lax.rem(me + k, ndev)
        pl.semaphore_signal(
            barrier,
            inc=1,
            device_id={"src": o // nrcv, "rcv": lax.rem(o, nrcv)},
            device_id_type=MESH,
        )
        return carry

    lax.fori_loop(1, ndev, greet, 0)

    def order(t):
        return jnp.where(t < half - 2, t + 1, jnp.where(t == half - 2, 0, half - 1))

    def at_position(h, n):
        return h * half + r * (half - 1) + n * (1 - 2 * r)

    def place(h, t):
        return at_position(h, order(t))

    tall = CHUNK + 2 * LANES
    k_ids = lax.broadcasted_iota(jnp.int32, (tall, CHUNK), 0) - LANES
    n_ids = lax.broadcasted_iota(jnp.int32, (tall, CHUNK), 1)
    band[...] = jnp.where((k_ids >= n_ids - HALF) & (k_ids <= n_ids + HALF), 1.0, 0.0).astype(bf16)

    zero = jnp.zeros((windows * local, LANES), bf16)
    outer = pl.ds(pl.multiple_of(r * (LANES + width), LANES), LANES)
    for buffer in (mag_hi, mag_lo):
        buffer[:, outer] = zero

    def turn_half(n, h):
        def turn_rows(c, carry):
            for w in range(windows):
                first = (w * 2 * tiles + h * 2 * per_half) * local
                rows = raw[n, c * windows + w].astype(f32)
                xt[pl.ds(first + c, 2 * per_half, stride=local), :] = rows
            return carry

        lax.fori_loop(0, local, turn_rows, 0, unroll=4)

    load_sent.wait()
    turn_half(0, 1 - par)

    def plane(w, tile, p):
        at = pl.multiple_of(((w * tiles + tile) * 2 + p) * local, 8)
        return xt[pl.ds(at, local), :]

    def magnitude(w, tile):
        re = plane(w, tile, 0)
        im = plane(w, tile, 1)
        m = jnp.sqrt(re * re + im * im)
        hi = m.astype(bf16)
        return hi, (m - hi.astype(f32)).astype(bf16)

    def magnitude_tile(tile):
        for w in range(windows):
            at = pl.ds(pl.multiple_of(LANES + tile * LANES, LANES), LANES)
            rows = pl.ds(w * local, local)
            mag_hi[rows, at], mag_lo[rows, at] = magnitude(w, tile)

    def magnitudes(j, carry):
        for d in range(CHUNK // LANES):
            magnitude_tile(j * (CHUNK // LANES) + d)
        return carry

    def inside(j):
        return jnp.minimum(jnp.maximum(j, 0), chunks - 1)

    def whiten(j):
        span = pl.ds(pl.multiple_of(j * CHUNK, LANES), tall)
        total = jnp.dot(mag_hi[:, span], band[...], preferred_element_type=f32)
        total = total + jnp.dot(mag_lo[:, span], band[...], preferred_element_type=f32)
        inverse = 1.0 / (total / (2 * HALF + 1) + smooth_eps)
        for w in range(windows):
            for d in range(CHUNK // LANES):
                lanes = slice(d * LANES, (d + 1) * LANES)
                part = inverse[w * local : (w + 1) * local, lanes]
                for p in range(2):
                    x = plane(w, j * (CHUNK // LANES) + d, p)
                    white[j, 2 * w + p, :, lanes] = (x * part).astype(bf16)

    partner = s + 1 - 2 * par
    beyond = s + 2 - 4 * par
    sends_far = (beyond >= 0) & (beyond < nsrc)
    back = s - 2 + 4 * par
    has_far = (back >= 0) & (back < nsrc)

    def near_copy(t, k):
        return pltpu.make_async_remote_copy(
            src_ref=white.at[place(1 - par, t), k],
            dst_ref=near.at[t, k],
            send_sem=near_send.at[t, k],
            recv_sem=near_recv.at[t, k],
            device_id={"src": partner},
            device_id_type=MESH,
        )

    def far_copy(t, k):
        return pltpu.make_async_remote_copy(
            src_ref=near.at[t, k],
            dst_ref=far.at[t, k],
            send_sem=far_send.at[t, k],
            recv_sem=far_recv.at[t, k],
            device_id={"src": beyond},
            device_id_type=MESH,
        )

    def direct_copy(u, k):
        return pltpu.make_async_remote_copy(
            src_ref=white.at[place(par, relayed + u), k],
            dst_ref=direct.at[u, k],
            send_sem=direct_send.at[u, k],
            recv_sem=direct_recv.at[u, k],
            device_id={"src": back},
            device_id_type=MESH,
        )


    def halo_copy(n):
        buffer = (mag_hi, mag_lo)[n]
        return pltpu.make_async_remote_copy(
            src_ref=edge_out.at[n],
            dst_ref=buffer.at[:, outer],
            send_sem=halo_send.at[n],
            recv_sem=halo_recv.at[n],
            device_id={"rcv": 1 - r},
            device_id_type=MESH,
        )

    def lab_copy(slot, to):
        return pltpu.make_async_remote_copy(
            src_ref=lab_out,
            dst_ref=lab_in.at[slot],
            send_sem=lab_send.at[slot],
            recv_sem=lab_recv.at[slot],
            device_id={"src": to},
            device_id_type=MESH,
        )

    sends_next = s + 1 < nsrc
    sends_second = (par == 1) & sends_next

    first_chunk = place(1 - par, 0)
    for d in range(-1, CHUNK // LANES + 1):
        magnitude_tile(first_chunk * (CHUNK // LANES) + d)
    whiten(first_chunk)
    load_labels.wait()
    labels = labels_ref[...]
    lab_out[...] = labels.astype(f32).astype(bf16)
    pl.semaphore_wait(barrier, ndev - 1)

    def send_near(t):
        for k in range(parts):
            near_copy(t, k).start()

    send_near(0)

    @pl.when(sends_next)
    def _():
        lab_copy(0, s + 1).start()

    @pl.when(sends_second)
    def _():
        lab_copy(1, s - 1).start()
        lab_copy(2, s + 2).start()

    load_kept.wait()
    turn_half(1, par)
    for w in range(windows):
        rows = pl.ds(w * local, local)
        edge_out[0, rows], edge_out[1, rows] = magnitude(w, (1 - r) * (tiles - 1))
    for n in range(2):
        halo_copy(n).start()

    def all_magnitudes(n, carry):
        return magnitudes(at_position(1 - par, n), carry)

    lax.fori_loop(0, half, all_magnitudes, 0)
    for n in (-1, half):
        magnitudes(inside(at_position(1 - par, n)), 0)

    def send_next(t, carry):
        whiten(place(1 - par, t))
        send_near(t)
        return carry

    lax.fori_loop(1, half - 1, send_next, 0)
    for n in range(2):
        halo_copy(n).wait_recv()
    whiten(place(1 - par, half - 1))
    send_near(half - 1)

    def keep_magnitude(t, carry):
        return magnitudes(place(par, t), carry)

    lax.fori_loop(0, half, keep_magnitude, 0)

    def keep_direct(u, carry):
        whiten(place(par, relayed + u))

        @pl.when(has_far)
        def _():
            for k in range(parts):
                direct_copy(u, k).start()

        return carry

    lax.fori_loop(0, half - relayed, keep_direct, 0)

    def keep(t, carry):
        whiten(place(par, t))
        return carry

    lax.fori_loop(0, relayed, keep, 0)

    lanes = count_out.shape[1]
    lane_ids = lax.broadcasted_iota(jnp.int32, (1, lanes), 1)
    valid = sends_next.astype(f32)

    def expand(b, counted):
        hits = jnp.where(labels == b, 1.0, 0.0).astype(f32)
        onehot[0, pl.ds(pl.multiple_of(b * local, 16), local), :] = hits.astype(bf16)
        found = jnp.sum(jnp.sum(hits, axis=0, keepdims=True), axis=1, keepdims=True)
        return counted + jnp.where(lane_ids == b, found, 0.0)

    counted = lax.fori_loop(0, nbins, expand, jnp.zeros((1, lanes), f32)) * valid
    count_out[...] = counted
    count_in[s] = counted

    def count_copy(o, slot):
        return pltpu.make_async_remote_copy(
            src_ref=count_out,
            dst_ref=count_in.at[slot],
            send_sem=count_send.at[o],
            recv_sem=count_recv.at[slot],
            device_id={"src": o},
            device_id_type=MESH,
        )

    def send_count(k, carry):
        count_copy(lax.rem(s + k, nsrc), s).start()
        return carry

    lax.fori_loop(1, nsrc, send_count, 0)

    def expand_into(which, table):
        def one(b, carry):
            onehot[which, pl.ds(pl.multiple_of(b * local, 16), local), :] = jnp.where(
                table == b, 1.0, 0.0
            ).astype(bf16)
            return carry

        lax.fori_loop(0, nbins, one, 0)

    @pl.when(s > 0)
    def _():
        lab_copy(0, s).wait_recv()
        expand_into(1, jnp.transpose(lab_in[0].astype(f32)).astype(jnp.int32))

    @pl.when(jnp.logical_not(sends_far))
    def _():
        onehot[2] = jnp.zeros((nbins * local, local), bf16)

    @pl.when(sends_far & (par == 0))
    def _():
        lab_copy(1, s).wait_recv()
        expand_into(2, jnp.transpose(lab_in[1].astype(f32)).astype(jnp.int32))

    @pl.when(sends_far & (par == 1))
    def _():
        lab_copy(2, s).wait_recv()
        expand_into(2, lab_in[2].astype(f32).astype(jnp.int32))

    load_owners.wait()
    owned = owners_ref[...]
    b_rows = lax.broadcasted_iota(jnp.int32, (nbins, nbins), 0)
    b_cols = lax.broadcasted_iota(jnp.int32, (nbins, nbins), 1)
    column = jnp.sum(jnp.where(b_rows == b_cols, owned, 0).astype(f32), axis=1, keepdims=True)
    earlier = jnp.where((column.astype(jnp.int32) == owned) & (b_rows < b_cols), 1.0, 0.0)
    slots = jnp.sum(earlier.astype(f32), axis=0, keepdims=True)
    rows_row = (owned.astype(f32) * CAP + slots).astype(jnp.int32)
    lines = CAP * 4
    cols = 4 * nbins
    tiled = jnp.concatenate([rows_row] * 4, axis=1)
    batch = 16
    row_ids = lax.broadcasted_iota(jnp.int32, (batch * lines, cols), 0)
    col_group = lax.broadcasted_iota(jnp.int32, (batch * lines, cols), 1) // nbins
    same_line = lax.rem(row_ids, 4) == col_group
    row_slot = row_ids // 4

    def prepare(g, carry):
        chosen = same_line & (tiled == row_slot + g * (batch * CAP))
        at = pl.ds(pl.multiple_of(g * (batch * lines), 16), batch * lines)
        pick[at] = jnp.where(chosen, 1.0, 0.0).astype(bf16)
        return carry

    lax.fori_loop(0, ndev // batch, prepare, 0)

    group = min(nbins, 16)

    def picks(which, g, other, t, w, slot):
        rows = group * local
        picked = onehot[which, pl.ds(pl.multiple_of(g * rows, 16), rows), :]
        for p in range(2):
            prod[slot + p] = jnp.dot(picked, other[t, 2 * w + p], preferred_element_type=f32)

    def add_products(sign, mine, g, t, slot):
        for b in range(group):
            rows = slice(b * local, (b + 1) * local)
            p_re, p_im = prod[slot, rows], prod[slot + 1, rows]
            o_re, o_im = mine[0], mine[1]
            re = (o_re * p_re + o_im * p_im).reshape(local // 8, 8, CHUNK)
            im = (o_im * p_re - o_re * p_im).reshape(local // 8, 8, CHUNK)
            acc[t, 0, g * group + b] += jnp.sum(re, axis=0)
            acc[t, 1, g * group + b] += jnp.sum(im, axis=0) * sign

    def take_own(t, w):
        for p in range(2):
            own[p] = white[place(par, t), 2 * w + p].astype(f32)

    sign_near = (1 - 2 * par).astype(f32)

    def part_copy(g, o, slot):
        return pltpu.make_async_remote_copy(
            src_ref=send_part.at[g, o],
            dst_ref=recv_part.at[g, slot],
            send_sem=part_send.at[g, o],
            recv_sem=part_recv.at[g, slot],
            device_id={"src": o // nrcv, "rcv": lax.rem(o, nrcv)},
            device_id_type=MESH,
        )

    def summed(t):
        rows = [
            jnp.sum(acc[t, q, :, :, d * LANES : (d + 1) * LANES], axis=1)
            for d in range(CHUNK // LANES)
            for q in range(2)
        ]
        return jnp.concatenate(rows, axis=0).astype(bf16)

    def route(g):
        stacked = [summed(2 * g + u) for u in range(2)]

        def some(q, carry):
            at = pl.ds(pl.multiple_of(q * (batch * lines), 16), batch * lines)
            wide = [jnp.dot(pick[at], rhs, preferred_element_type=f32) for rhs in stacked]
            for n in range(batch):
                both = [v[n * lines : (n + 1) * lines] for v in wide]
                send_part[g, q * batch + n] = jnp.concatenate(both, axis=0).astype(bf16)
            return carry

        lax.fori_loop(0, ndev // batch, some, 0)

        def send_one(k, carry):
            part_copy(g, lax.rem(me + k, ndev), me).start()
            return carry

        lax.fori_loop(1, ndev, send_one, 0)
        recv_part[g, me] = send_part[g, me]

    acc[...] = jnp.zeros(acc.shape, f32)

    def far_piece(q):
        t, w = q // windows, lax.rem(q, windows)
        for p in range(2):
            far_copy(t, 2 * w + p).wait_recv()
        take_own(t, w)

        def some(g, carry):
            picks(1 - par, g, far, t, w, 0)
            add_products(-sign_near, own, g, t, 0)
            return carry

        lax.fori_loop(0, nbins // group, some, 0)

    def relay_piece(q, carry):
        t, w = q // windows, lax.rem(q, windows)
        for p in range(2):
            near_copy(t, 2 * w + p).wait_recv()

            @pl.when(sends_far)
            def _():
                far_copy(t, 2 * w + p).start()

        take_own(t, w)

        def some(g, carry):
            picks(par, g, near, t, w, 0)
            add_products(sign_near, own, g, t, 0)
            return carry

        lax.fori_loop(0, nbins // group, some, 0)

        return carry

    lax.fori_loop(0, relayed * windows, relay_piece, 0)

    @pl.when(sends_far)
    def _():
        for u in range(half - relayed):
            for k in range(parts):
                direct_copy(u, k).wait_recv()

    def direct_piece(q, carry):
        t, w = q // windows, lax.rem(q, windows)
        take_own(t, w)

        @pl.when(sends_far)
        def _():
            for p in range(2):
                own_d[p] = direct[t - relayed, 2 * w + p].astype(f32)

        for p in range(2):
            near_copy(t, 2 * w + p).wait_recv()

        def some(g, carry):
            picks(par, g, near, t, w, 0)
            picks(2, g, near, t, w, 2)
            add_products(sign_near, own, g, t, 0)
            add_products(-sign_near, own_d, g, t, 2)
            return carry

        lax.fori_loop(0, nbins // group, some, 0)

        @pl.when(has_far & (t == relayed))
        def _():
            def some_far(n, inner):
                far_piece(w * relayed + n)
                return inner

            lax.fori_loop(0, relayed, some_far, 0)

        @pl.when((t == relayed) & (w == windows - 1))
        def _():
            route(0)

        return carry

    own_d[...] = jnp.zeros(own_d.shape, f32)
    lax.fori_loop(relayed * windows, half * windows, direct_piece, 0)

    route(1)

    def take_count(k, carry):
        o = lax.rem(s + k, nsrc)
        count_copy(o, o).wait_recv()
        return carry

    lax.fori_loop(1, nsrc, take_count, 0)
    counts = jnp.sum(count_in[...], axis=0)[0:1, :nbins]
    scale = []
    for c in range(CAP):
        mine = jnp.sum(jnp.where(rows_row == me * CAP + c, counts, 0.0), axis=1, keepdims=True)
        scale.append(1.0 / jnp.sqrt(jnp.maximum(mine, 1.0)))
    for g in range(half // 2):

        def take_part(k, carry):
            o = lax.rem(me + k, ndev)
            part_copy(g, o, o).wait_recv()
            return carry

        lax.fori_loop(1, ndev, take_part, 0)
        for rr in range(nrcv):
            for pp in range(2):

                def add(z, total):
                    return total + recv_part[g, (2 * z + pp) * nrcv + rr].astype(f32)

                total = lax.fori_loop(0, nsrc // 2, add, jnp.zeros((2 * lines, LANES), f32))
                for u in range(2):
                    t = 2 * g + u
                    n = t + 1 if t < half - 2 else 0 if t == half - 2 else half - 1
                    j = pp * half + rr * (half - 1) + n * (1 - 2 * rr)
                    for c in range(CAP):
                        row = (c * nrcv * chunks + rr * chunks + j) * 4
                        value = total[u * lines + c * 4 : u * lines + c * 4 + 4]
                        out_ref[row : row + 4] = value * scale[c]

    for t in range(half):
        for k in range(parts):
            near_copy(t, k).wait_send()

    @pl.when(sends_far)
    def _():
        for t in range(relayed):
            for k in range(parts):
                far_copy(t, k).wait_send()

    @pl.when(has_far)
    def _():
        for u in range(half - relayed):
            for k in range(parts):
                direct_copy(u, k).wait_send()

    for n in range(2):
        halo_copy(n).wait_send()

    @pl.when(sends_next)
    def _():
        lab_copy(0, s + 1).wait_send()

    @pl.when(sends_second)
    def _():
        lab_copy(1, s - 1).wait_send()
        lab_copy(2, s + 2).wait_send()

    def end_count(k, carry):
        count_copy(lax.rem(s + k, nsrc), s).wait_send()
        return carry

    lax.fori_loop(1, nsrc, end_count, 0)

    def end_part(k, carry):
        for g in range(half // 2):
            part_copy(g, lax.rem(me + k, ndev), me).wait_send()
        return carry

    lax.fori_loop(1, ndev, end_part, 0)


def per_device(spectra, pair_bins, owners):
    local, windows, _, width = spectra.shape
    nbins = owners.shape[0]
    nsrc = lax.axis_size("src")
    nrcv = lax.axis_size("rcv")
    ndev = nsrc * nrcv
    chunks = width // CHUNK
    half = chunks // 2
    relayed = half // 2
    tiles = width // LANES
    parts = 2 * windows
    lanes = -(-nbins // 128) * 128
    group = min(nbins, 16)
    x = spectra.reshape(local * windows, 2, tiles, LANES).transpose(0, 2, 1, 3)
    x = x.reshape(local * windows, 2 * tiles, LANES)
    dims = (nsrc, nrcv, nbins, local, windows, chunks)
    bf16, f32 = jnp.bfloat16, jnp.float32
    dma = pltpu.SemaphoreType.DMA
    hbm = pl.BlockSpec(memory_space=pltpu.HBM)
    args = [
        pltpu.with_memory_space_constraint(v, pltpu.HBM) for v in (x, pair_bins, owners[None])
    ]
    out = pl.pallas_call(
        functools.partial(kernel, dims),
        out_shape=jax.ShapeDtypeStruct((CAP * nrcv * tiles * 2, LANES), f32),
        in_specs=[hbm] * 3,
        out_specs=pl.BlockSpec(memory_space=pltpu.VMEM),
        scratch_shapes=[
            pltpu.VMEM((2, local * windows, tiles, LANES), bf16),
            pltpu.VMEM((windows * 2 * tiles * local, LANES), f32),
            pltpu.VMEM((chunks, parts, local, CHUNK), bf16),
            pltpu.VMEM((half, parts, local, CHUNK), bf16),
            pltpu.VMEM((relayed, parts, local, CHUNK), bf16),
            pltpu.VMEM((half - relayed, parts, local, CHUNK), bf16),
            pltpu.VMEM((windows * local, width + 2 * LANES), bf16),
            pltpu.VMEM((windows * local, width + 2 * LANES), bf16),
            pltpu.VMEM((2, windows * local, LANES), bf16),
            pltpu.VMEM((CHUNK + 2 * LANES, CHUNK), bf16),
            pltpu.VMEM((3, nbins * local, local), bf16),
            pltpu.VMEM((2, local, CHUNK), f32),
            pltpu.VMEM((2, local, CHUNK), f32),
            pltpu.VMEM((4, group * local, CHUNK), f32),
            pltpu.VMEM((half, 2, nbins, 8, CHUNK), f32),
            pltpu.VMEM((ndev * CAP * 4, 4 * nbins), bf16),
            pltpu.VMEM((half // 2, ndev, CAP * 8, LANES), bf16),
            pltpu.VMEM((half // 2, ndev, CAP * 8, LANES), bf16),
            pltpu.VMEM((local, local), jnp.int32),
            pltpu.VMEM((1, nbins), jnp.int32),
            pltpu.VMEM((local, local), bf16),
            pltpu.VMEM((3, local, local), bf16),
            pltpu.VMEM((1, lanes), f32),
            pltpu.VMEM((nsrc, 1, lanes), f32),
            dma((4,)),
            dma((half, parts)),
            dma((half, parts)),
            dma((relayed, parts)),
            dma((relayed, parts)),
            dma((half - relayed, parts)),
            dma((half - relayed, parts)),
            dma((2,)),
            dma((2,)),
            dma((3,)),
            dma((3,)),
            dma((nsrc,)),
            dma((nsrc,)),
            dma((half // 2, ndev)),
            dma((half // 2, ndev)),
        ],
        compiler_params=pltpu.CompilerParams(
            collective_id=0, has_side_effects=True, vmem_limit_bytes=48 * 1024 * 1024
        ),
    )(*args)
    out = out.reshape(CAP, nrcv * tiles, 2, LANES).transpose(0, 2, 1, 3)
    return out.reshape(CAP, 2, nrcv * width)


def solution(mesh):
    in_specs = (P(("groups", "src"), None, None, "rcv"), P(("groups", "src"), None), P("groups"))
    out_specs = P(("groups", "src", "rcv"), None, None)
    return jax.shard_map(
        per_device, mesh=mesh, in_specs=in_specs, out_specs=out_specs, check_vma=False
    )
```

```python
import functools

import jax
import jax.numpy as jnp
from jax import lax
from jax.experimental import pallas as pl
from jax.experimental.pallas import tpu as pltpu
from jax.sharding import PartitionSpec as P

HALF = 32
CAP = 2
LANES = 128
CHUNK = 256
smooth_eps = 1e-06
MESH = pl.DeviceIdType.MESH


def kernel(
    dims,
    x_hbm,
    lab_hbm,
    owners_hbm,
    out_ref,
    raw,
    xt,
    white,
    near,
    far,
    direct,
    mag_hi,
    mag_lo,
    edge_out,
    band,
    onehot,
    own,
    own_d,
    prod,
    acc,
    pick,
    send_most,
    recv_most,
    send_last,
    recv_last,
    labels_ref,
    owners_ref,
    lab_out,
    lab_in,
    count_out,
    count_in,
    load_sems,
    near_send,
    near_recv,
    far_send,
    far_recv,
    direct_send,
    direct_recv,
    halo_send,
    halo_recv,
    lab_send,
    lab_recv,
    count_send,
    count_recv,
    part_send,
    part_recv,
):
    nsrc, nrcv, nbins, local, windows, chunks = dims
    half = chunks // 2
    relayed = half // 2
    parts = 2 * windows
    width = chunks * CHUNK
    tiles = width // LANES
    per_half = tiles // 2
    ndev = nsrc * nrcv
    s = lax.axis_index("src")
    r = lax.axis_index("rcv")
    me = s * nrcv + r
    par = lax.rem(s, 2)
    f32 = jnp.float32
    bf16 = jnp.bfloat16

    def load_half(n, h):
        rows = pl.ds(pl.multiple_of(h * 2 * per_half, 16), 2 * per_half)
        return pltpu.make_async_copy(x_hbm.at[:, rows], raw.at[n], load_sems.at[n])

    load_sent = load_half(0, 1 - par)
    load_kept = load_half(1, par)
    load_labels = pltpu.make_async_copy(lab_hbm, labels_ref, load_sems.at[2])
    load_owners = pltpu.make_async_copy(owners_hbm, owners_ref, load_sems.at[3])
    for load in (load_sent, load_labels, load_kept, load_owners):
        load.start()

    barrier = pltpu.get_barrier_semaphore()

    def greet(k, carry):
        o = lax.rem(me + k, ndev)
        pl.semaphore_signal(
            barrier,
            inc=1,
            device_id={"src": o // nrcv, "rcv": lax.rem(o, nrcv)},
            device_id_type=MESH,
        )
        return carry

    lax.fori_loop(1, ndev, greet, 0)

    def order(t):
        return jnp.where(t < half - 2, t + 1, jnp.where(t == half - 2, 0, half - 1))

    def at_position(h, n):
        return h * half + r * (half - 1) + n * (1 - 2 * r)

    def place(h, t):
        return at_position(h, order(t))

    tall = CHUNK + 2 * LANES
    k_ids = lax.broadcasted_iota(jnp.int32, (tall, CHUNK), 0) - LANES
    n_ids = lax.broadcasted_iota(jnp.int32, (tall, CHUNK), 1)
    band[...] = jnp.where((k_ids >= n_ids - HALF) & (k_ids <= n_ids + HALF), 1.0, 0.0).astype(bf16)

    zero = jnp.zeros((windows * local, LANES), bf16)
    outer = pl.ds(pl.multiple_of(r * (LANES + width), LANES), LANES)
    for buffer in (mag_hi, mag_lo):
        buffer[:, outer] = zero

    def turn_half(n, h):
        def turn_rows(c, carry):
            for w in range(windows):
                first = (w * 2 * tiles + h * 2 * per_half) * local
                rows = raw[n, c * windows + w].astype(f32)
                xt[pl.ds(first + c, 2 * per_half, stride=local), :] = rows
            return carry

        lax.fori_loop(0, local, turn_rows, 0, unroll=4)

    load_sent.wait()
    turn_half(0, 1 - par)

    def plane(w, tile, p):
        at = pl.multiple_of(((w * tiles + tile) * 2 + p) * local, 8)
        return xt[pl.ds(at, local), :]

    def magnitude(w, tile):
        re = plane(w, tile, 0)
        im = plane(w, tile, 1)
        m = jnp.sqrt(re * re + im * im)
        hi = m.astype(bf16)
        return hi, (m - hi.astype(f32)).astype(bf16)

    def magnitude_tile(tile):
        for w in range(windows):
            at = pl.ds(pl.multiple_of(LANES + tile * LANES, LANES), LANES)
            rows = pl.ds(w * local, local)
            mag_hi[rows, at], mag_lo[rows, at] = magnitude(w, tile)

    def magnitudes(j, carry):
        for d in range(CHUNK // LANES):
            magnitude_tile(j * (CHUNK // LANES) + d)
        return carry

    def inside(j):
        return jnp.minimum(jnp.maximum(j, 0), chunks - 1)

    def whiten(j):
        span = pl.ds(pl.multiple_of(j * CHUNK, LANES), tall)
        total = jnp.dot(mag_hi[:, span], band[...], preferred_element_type=f32)
        total = total + jnp.dot(mag_lo[:, span], band[...], preferred_element_type=f32)
        inverse = 1.0 / (total / (2 * HALF + 1) + smooth_eps)
        for w in range(windows):
            for d in range(CHUNK // LANES):
                lanes = slice(d * LANES, (d + 1) * LANES)
                part = inverse[w * local : (w + 1) * local, lanes]
                for p in range(2):
                    x = plane(w, j * (CHUNK // LANES) + d, p)
                    white[j, 2 * w + p, :, lanes] = (x * part).astype(bf16)

    partner = s + 1 - 2 * par
    beyond = s + 2 - 4 * par
    sends_far = (beyond >= 0) & (beyond < nsrc)
    back = s - 2 + 4 * par
    has_far = (back >= 0) & (back < nsrc)

    def near_copy(t, k):
        return pltpu.make_async_remote_copy(
            src_ref=white.at[place(1 - par, t), k],
            dst_ref=near.at[t, k],
            send_sem=near_send.at[t, k],
            recv_sem=near_recv.at[t, k],
            device_id={"src": partner},
            device_id_type=MESH,
        )

    def far_copy(t, k):
        return pltpu.make_async_remote_copy(
            src_ref=near.at[t, k],
            dst_ref=far.at[t, k],
            send_sem=far_send.at[t, k],
            recv_sem=far_recv.at[t, k],
            device_id={"src": beyond},
            device_id_type=MESH,
        )

    def direct_copy(u, k):
        return pltpu.make_async_remote_copy(
            src_ref=white.at[place(par, relayed + u), k],
            dst_ref=direct.at[u, k],
            send_sem=direct_send.at[u, k],
            recv_sem=direct_recv.at[u, k],
            device_id={"src": back},
            device_id_type=MESH,
        )


    def halo_copy(n):
        buffer = (mag_hi, mag_lo)[n]
        return pltpu.make_async_remote_copy(
            src_ref=edge_out.at[n],
            dst_ref=buffer.at[:, outer],
            send_sem=halo_send.at[n],
            recv_sem=halo_recv.at[n],
            device_id={"rcv": 1 - r},
            device_id_type=MESH,
        )

    def lab_copy(slot, to):
        return pltpu.make_async_remote_copy(
            src_ref=lab_out,
            dst_ref=lab_in.at[slot],
            send_sem=lab_send.at[slot],
            recv_sem=lab_recv.at[slot],
            device_id={"src": to},
            device_id_type=MESH,
        )

    label_pass = pltpu.make_async_remote_copy(
        src_ref=lab_in.at[1],
        dst_ref=lab_in.at[0],
        send_sem=lab_send.at[2],
        recv_sem=lab_recv.at[0],
        device_id={"src": s + 2},
        device_id_type=MESH,
    )

    sends_next = s + 1 < nsrc
    sends_label = (par == 0) & sends_next
    sends_second = (par == 1) & sends_next
    passes_label = (par == 0) & sends_far

    first_chunk = place(1 - par, 0)
    for d in range(-1, CHUNK // LANES + 1):
        magnitude_tile(first_chunk * (CHUNK // LANES) + d)
    whiten(first_chunk)
    pl.semaphore_wait(barrier, ndev - 1)

    def send_near(t):
        for k in range(parts):
            near_copy(t, k).start()

    send_near(0)

    load_labels.wait()
    labels = labels_ref[...]
    lab_out[...] = labels.astype(f32).astype(bf16)

    @pl.when(sends_label)
    def _():
        lab_copy(0, s + 1).start()

    @pl.when(sends_second)
    def _():
        lab_copy(1, s - 1).start()
        lab_copy(2, s + 2).start()

    load_kept.wait()
    turn_half(1, par)
    for w in range(windows):
        rows = pl.ds(w * local, local)
        edge_out[0, rows], edge_out[1, rows] = magnitude(w, (1 - r) * (tiles - 1))
    for n in range(2):
        halo_copy(n).start()

    def all_magnitudes(n, carry):
        return magnitudes(at_position(1 - par, n), carry)

    lax.fori_loop(0, half, all_magnitudes, 0)
    for n in (-1, half):
        magnitudes(inside(at_position(1 - par, n)), 0)

    def send_next(t, carry):
        whiten(place(1 - par, t))
        send_near(t)
        return carry

    lax.fori_loop(1, half - 1, send_next, 0)
    for n in range(2):
        halo_copy(n).wait_recv()
    whiten(place(1 - par, half - 1))
    send_near(half - 1)

    def keep_magnitude(t, carry):
        return magnitudes(place(par, t), carry)

    lax.fori_loop(0, half, keep_magnitude, 0)

    def keep_direct(u, carry):
        whiten(place(par, relayed + u))

        @pl.when(has_far)
        def _():
            for k in range(parts):
                direct_copy(u, k).start()

        return carry

    lax.fori_loop(0, half - relayed, keep_direct, 0)

    def keep(t, carry):
        whiten(place(par, t))
        return carry

    lax.fori_loop(0, relayed, keep, 0)

    lanes = count_out.shape[1]
    lane_ids = lax.broadcasted_iota(jnp.int32, (1, lanes), 1)
    valid = sends_next.astype(f32)

    def expand(b, counted):
        hits = jnp.where(labels == b, 1.0, 0.0).astype(f32)
        onehot[0, pl.ds(pl.multiple_of(b * local, 16), local), :] = hits.astype(bf16)
        found = jnp.sum(jnp.sum(hits, axis=0, keepdims=True), axis=1, keepdims=True)
        return counted + jnp.where(lane_ids == b, found, 0.0)

    counted = lax.fori_loop(0, nbins, expand, jnp.zeros((1, lanes), f32)) * valid
    count_out[...] = counted
    count_in[s] = counted

    def count_copy(o, slot):
        return pltpu.make_async_remote_copy(
            src_ref=count_out,
            dst_ref=count_in.at[slot],
            send_sem=count_send.at[o],
            recv_sem=count_recv.at[slot],
            device_id={"src": o},
            device_id_type=MESH,
        )

    def send_count(k, carry):
        count_copy(lax.rem(s + k, nsrc), s).start()
        return carry

    lax.fori_loop(1, nsrc, send_count, 0)

    def expand_into(which, table):
        def one(b, carry):
            onehot[which, pl.ds(pl.multiple_of(b * local, 16), local), :] = jnp.where(
                table == b, 1.0, 0.0
            ).astype(bf16)
            return carry

        lax.fori_loop(0, nbins, one, 0)

    @pl.when(par == 1)
    def _():
        lab_copy(0, s).wait_recv()
        expand_into(1, jnp.transpose(lab_in[0].astype(f32)).astype(jnp.int32))

    @pl.when(jnp.logical_not(sends_far))
    def _():
        onehot[2] = jnp.zeros((nbins * local, local), bf16)

    @pl.when(passes_label)
    def _():
        lab_copy(1, s).wait_recv()
        label_pass.start()
        expand_into(2, jnp.transpose(lab_in[1].astype(f32)).astype(jnp.int32))

    @pl.when(sends_far & (par == 1))
    def _():
        lab_copy(2, s).wait_recv()
        expand_into(2, lab_in[2].astype(f32).astype(jnp.int32))

    load_owners.wait()
    owned = owners_ref[...]
    b_rows = lax.broadcasted_iota(jnp.int32, (nbins, nbins), 0)
    b_cols = lax.broadcasted_iota(jnp.int32, (nbins, nbins), 1)
    column = jnp.sum(jnp.where(b_rows == b_cols, owned, 0).astype(f32), axis=1, keepdims=True)
    earlier = jnp.where((column.astype(jnp.int32) == owned) & (b_rows < b_cols), 1.0, 0.0)
    slots = jnp.sum(earlier.astype(f32), axis=0, keepdims=True)
    rows_row = (owned.astype(f32) * CAP + slots).astype(jnp.int32)
    lines = CAP * 4
    cols = 4 * nbins
    tiled = jnp.concatenate([rows_row] * 4, axis=1)
    batch = 16
    row_ids = lax.broadcasted_iota(jnp.int32, (batch * lines, cols), 0)
    col_group = lax.broadcasted_iota(jnp.int32, (batch * lines, cols), 1) // nbins
    same_line = lax.rem(row_ids, 4) == col_group
    row_slot = row_ids // 4

    def prepare(g, carry):
        chosen = same_line & (tiled == row_slot + g * (batch * CAP))
        at = pl.ds(pl.multiple_of(g * (batch * lines), 16), batch * lines)
        pick[at] = jnp.where(chosen, 1.0, 0.0).astype(bf16)
        return carry

    lax.fori_loop(0, ndev // batch, prepare, 0)

    group = min(nbins, 16)

    def pick_one(which, g, other, t, w, p, slot):
        rows = group * local
        picked = onehot[which, pl.ds(pl.multiple_of(g * rows, 16), rows), :]
        prod[slot + p] = jnp.dot(picked, other[t, 2 * w + p], preferred_element_type=f32)

    def picks(which, g, other, t, w, slot):
        for p in range(2):
            pick_one(which, g, other, t, w, p, slot)

    def add_products(sign, mine, g, t, slot):
        for b in range(group):
            rows = slice(b * local, (b + 1) * local)
            p_re, p_im = prod[slot, rows], prod[slot + 1, rows]
            o_re, o_im = mine[0], mine[1]
            re = (o_re * p_re + o_im * p_im).reshape(local // 8, 8, CHUNK)
            im = (o_im * p_re - o_re * p_im).reshape(local // 8, 8, CHUNK)
            acc[t, 0, g * group + b] += jnp.sum(re, axis=0)
            acc[t, 1, g * group + b] += jnp.sum(im, axis=0) * sign

    def take_own(t, w):
        for p in range(2):
            own[p] = white[place(par, t), 2 * w + p].astype(f32)

    sign_near = (1 - 2 * par).astype(f32)

    rounds = ((0, half - 1, send_most, recv_most), (half - 1, half, send_last, recv_last))

    def part_copy(g, o, slot):
        _, _, out_part, in_part = rounds[g]
        return pltpu.make_async_remote_copy(
            src_ref=out_part.at[o],
            dst_ref=in_part.at[slot],
            send_sem=part_send.at[g, o],
            recv_sem=part_recv.at[g, slot],
            device_id={"src": o // nrcv, "rcv": lax.rem(o, nrcv)},
            device_id_type=MESH,
        )

    def summed(t):
        rows = [
            jnp.sum(acc[t, q, :, :, d * LANES : (d + 1) * LANES], axis=1)
            for d in range(CHUNK // LANES)
            for q in range(2)
        ]
        return jnp.concatenate(rows, axis=0).astype(bf16)

    def route(g):
        first, last, out_part, in_part = rounds[g]
        for t in range(first, last):
            wide = jnp.dot(pick[...], summed(t), preferred_element_type=f32)
            out_part[:, t - first] = wide.reshape(ndev, lines, LANES).astype(bf16)

        def send_one(k, carry):
            part_copy(g, lax.rem(me + k, ndev), me).start()
            return carry

        lax.fori_loop(1, ndev, send_one, 0)
        in_part[me] = out_part[me]

    acc[...] = jnp.zeros(acc.shape, f32)

    def far_piece(q):
        t, w = q // windows, lax.rem(q, windows)
        for p in range(2):
            far_copy(t, 2 * w + p).wait_recv()
        take_own(t, w)

        def some(g, carry):
            picks(1 - par, g, far, t, w, 0)
            add_products(-sign_near, own, g, t, 0)
            return carry

        lax.fori_loop(0, nbins // group, some, 0)

    def relay_piece(q, carry):
        t, w = q // windows, lax.rem(q, windows)
        for p in range(2):
            near_copy(t, 2 * w + p).wait_recv()

            @pl.when(sends_far)
            def _():
                far_copy(t, 2 * w + p).start()

        take_own(t, w)

        def some(g, carry):
            picks(par, g, near, t, w, 0)
            add_products(sign_near, own, g, t, 0)
            return carry

        lax.fori_loop(0, nbins // group, some, 0)

        return carry

    lax.fori_loop(0, relayed * windows, relay_piece, 0)

    @pl.when((par == 0) & has_far)
    def _():
        lab_copy(0, s).wait_recv()
        expand_into(1, jnp.transpose(lab_in[0].astype(f32)).astype(jnp.int32))

    @pl.when(sends_far)
    def _():
        for u in range(half - relayed):
            for k in range(parts):
                direct_copy(u, k).wait_recv()

    def direct_piece(q, carry):
        t, w = q // windows, lax.rem(q, windows)
        take_own(t, w)

        @pl.when(sends_far)
        def _():
            for p in range(2):
                own_d[p] = direct[t - relayed, 2 * w + p].astype(f32)

        for p in range(2):
            near_copy(t, 2 * w + p).wait_recv()

        def some(g, carry):
            picks(par, g, near, t, w, 0)
            picks(2, g, near, t, w, 2)
            add_products(sign_near, own, g, t, 0)
            add_products(-sign_near, own_d, g, t, 2)
            return carry

        lax.fori_loop(0, nbins // group, some, 0)

        @pl.when(has_far & (t == relayed))
        def _():
            def some_far(n, inner):
                far_piece(w * relayed + n)
                return inner

            lax.fori_loop(0, relayed, some_far, 0)

        @pl.when((t == half - 2) & (w == windows - 1))
        def _():
            route(0)

        return carry

    own_d[...] = jnp.zeros(own_d.shape, f32)
    lax.fori_loop(relayed * windows, half * windows, direct_piece, 0)

    route(1)

    def take_count(k, carry):
        o = lax.rem(s + k, nsrc)
        count_copy(o, o).wait_recv()
        return carry

    lax.fori_loop(1, nsrc, take_count, 0)
    counts = jnp.sum(count_in[...], axis=0)[0:1, :nbins]
    scale = []
    for c in range(CAP):
        mine = jnp.sum(jnp.where(rows_row == me * CAP + c, counts, 0.0), axis=1, keepdims=True)
        scale.append(1.0 / jnp.sqrt(jnp.maximum(mine, 1.0)))
    for g in range(2):
        first, last, _, in_part = rounds[g]

        def take_part(k, carry):
            o = lax.rem(me + k, ndev)
            part_copy(g, o, o).wait_recv()
            return carry

        lax.fori_loop(1, ndev, take_part, 0)
        for rr in range(nrcv):
            for pp in range(2):

                def add(z, total):
                    return total + in_part[(2 * z + pp) * nrcv + rr].astype(f32)

                total = jnp.zeros((last - first, lines, LANES), f32)
                total = lax.fori_loop(0, nsrc // 2, add, total)
                for t in range(first, last):
                    n = t + 1 if t < half - 2 else 0 if t == half - 2 else half - 1
                    j = pp * half + rr * (half - 1) + n * (1 - 2 * rr)
                    for c in range(CAP):
                        row = (c * nrcv * chunks + rr * chunks + j) * 4
                        out_ref[row : row + 4] = total[t - first, c * 4 : c * 4 + 4] * scale[c]

    for t in range(half):
        for k in range(parts):
            near_copy(t, k).wait_send()

    @pl.when(sends_far)
    def _():
        for t in range(relayed):
            for k in range(parts):
                far_copy(t, k).wait_send()

    @pl.when(has_far)
    def _():
        for u in range(half - relayed):
            for k in range(parts):
                direct_copy(u, k).wait_send()

    for n in range(2):
        halo_copy(n).wait_send()

    @pl.when(sends_label)
    def _():
        lab_copy(0, s + 1).wait_send()

    @pl.when(passes_label)
    def _():
        label_pass.wait_send()

    @pl.when(sends_second)
    def _():
        lab_copy(1, s - 1).wait_send()
        lab_copy(2, s + 2).wait_send()

    def end_count(k, carry):
        count_copy(lax.rem(s + k, nsrc), s).wait_send()
        return carry

    lax.fori_loop(1, nsrc, end_count, 0)

    def end_part(k, carry):
        for g in range(2):
            part_copy(g, lax.rem(me + k, ndev), me).wait_send()
        return carry

    lax.fori_loop(1, ndev, end_part, 0)


def per_device(spectra, pair_bins, owners):
    local, windows, _, width = spectra.shape
    nbins = owners.shape[0]
    nsrc = lax.axis_size("src")
    nrcv = lax.axis_size("rcv")
    ndev = nsrc * nrcv
    chunks = width // CHUNK
    half = chunks // 2
    relayed = half // 2
    tiles = width // LANES
    parts = 2 * windows
    lanes = -(-nbins // 128) * 128
    group = min(nbins, 16)
    x = spectra.reshape(local * windows, 2, tiles, LANES).transpose(0, 2, 1, 3)
    x = x.reshape(local * windows, 2 * tiles, LANES)
    dims = (nsrc, nrcv, nbins, local, windows, chunks)
    bf16, f32 = jnp.bfloat16, jnp.float32
    dma = pltpu.SemaphoreType.DMA
    hbm = pl.BlockSpec(memory_space=pltpu.HBM)
    args = [
        pltpu.with_memory_space_constraint(v, pltpu.HBM) for v in (x, pair_bins, owners[None])
    ]
    out = pl.pallas_call(
        functools.partial(kernel, dims),
        out_shape=jax.ShapeDtypeStruct((CAP * nrcv * tiles * 2, LANES), f32),
        in_specs=[hbm] * 3,
        out_specs=pl.BlockSpec(memory_space=pltpu.VMEM),
        scratch_shapes=[
            pltpu.VMEM((2, local * windows, tiles, LANES), bf16),
            pltpu.VMEM((windows * 2 * tiles * local, LANES), f32),
            pltpu.VMEM((chunks, parts, local, CHUNK), bf16),
            pltpu.VMEM((half, parts, local, CHUNK), bf16),
            pltpu.VMEM((relayed, parts, local, CHUNK), bf16),
            pltpu.VMEM((half - relayed, parts, local, CHUNK), bf16),
            pltpu.VMEM((windows * local, width + 2 * LANES), bf16),
            pltpu.VMEM((windows * local, width + 2 * LANES), bf16),
            pltpu.VMEM((2, windows * local, LANES), bf16),
            pltpu.VMEM((CHUNK + 2 * LANES, CHUNK), bf16),
            pltpu.VMEM((3, nbins * local, local), bf16),
            pltpu.VMEM((2, local, CHUNK), f32),
            pltpu.VMEM((2, local, CHUNK), f32),
            pltpu.VMEM((4, group * local, CHUNK), f32),
            pltpu.VMEM((half, 2, nbins, 8, CHUNK), f32),
            pltpu.VMEM((ndev * CAP * 4, 4 * nbins), bf16),
            pltpu.VMEM((ndev, half - 1, CAP * 4, LANES), bf16),
            pltpu.VMEM((ndev, half - 1, CAP * 4, LANES), bf16),
            pltpu.VMEM((ndev, 1, CAP * 4, LANES), bf16),
            pltpu.VMEM((ndev, 1, CAP * 4, LANES), bf16),
            pltpu.VMEM((local, local), jnp.int32),
            pltpu.VMEM((1, nbins), jnp.int32),
            pltpu.VMEM((local, local), bf16),
            pltpu.VMEM((3, local, local), bf16),
            pltpu.VMEM((1, lanes), f32),
            pltpu.VMEM((nsrc, 1, lanes), f32),
            dma((4,)),
            dma((half, parts)),
            dma((half, parts)),
            dma((relayed, parts)),
            dma((relayed, parts)),
            dma((half - relayed, parts)),
            dma((half - relayed, parts)),
            dma((2,)),
            dma((2,)),
            dma((3,)),
            dma((3,)),
            dma((nsrc,)),
            dma((nsrc,)),
            dma((2, ndev)),
            dma((2, ndev)),
        ],
        compiler_params=pltpu.CompilerParams(
            collective_id=0, has_side_effects=True, vmem_limit_bytes=48 * 1024 * 1024
        ),
    )(*args)
    out = out.reshape(CAP, nrcv * tiles, 2, LANES).transpose(0, 2, 1, 3)
    return out.reshape(CAP, 2, nrcv * width)


def solution(mesh):
    in_specs = (P(("groups", "src"), None, None, "rcv"), P(("groups", "src"), None), P("groups"))
    out_specs = P(("groups", "src", "rcv"), None, None)
    return jax.shard_map(
        per_device, mesh=mesh, in_specs=in_specs, out_specs=out_specs, check_vma=False
    )
```

```python
import functools

import jax
import jax.numpy as jnp
from jax import lax
from jax.experimental import pallas as pl
from jax.experimental.pallas import tpu as pltpu
from jax.sharding import PartitionSpec as P

HALF = 32
CAP = 2
LANES = 128
CHUNK = 256
smooth_eps = 1e-06
MESH = pl.DeviceIdType.MESH


def kernel(
    dims,
    x_hbm,
    lab_hbm,
    owners_hbm,
    out_ref,
    raw,
    xt,
    white,
    near,
    far,
    direct,
    mag_hi,
    mag_lo,
    edge_out,
    band,
    onehot,
    own,
    own_d,
    prod,
    acc,
    pick,
    send_part,
    recv_part,
    labels_ref,
    owners_ref,
    lab_out,
    lab_in,
    count_out,
    count_in,
    load_sems,
    near_send,
    near_recv,
    far_send,
    far_recv,
    direct_send,
    direct_recv,
    halo_send,
    halo_recv,
    lab_send,
    lab_recv,
    count_send,
    count_recv,
    part_send,
    part_recv,
):
    nsrc, nrcv, nbins, local, windows, chunks = dims
    half = chunks // 2
    relayed = half // 2
    parts = 2 * windows
    width = chunks * CHUNK
    tiles = width // LANES
    per_half = tiles // 2
    ndev = nsrc * nrcv
    s = lax.axis_index("src")
    r = lax.axis_index("rcv")
    me = s * nrcv + r
    par = lax.rem(s, 2)
    f32 = jnp.float32
    bf16 = jnp.bfloat16

    def load_half(n, h):
        rows = pl.ds(pl.multiple_of(h * 2 * per_half, 16), 2 * per_half)
        return pltpu.make_async_copy(x_hbm.at[:, rows], raw.at[n], load_sems.at[n])

    load_sent = load_half(0, 1 - par)
    load_kept = load_half(1, par)
    load_labels = pltpu.make_async_copy(lab_hbm, labels_ref, load_sems.at[2])
    load_owners = pltpu.make_async_copy(owners_hbm, owners_ref, load_sems.at[3])
    for load in (load_sent, load_labels, load_kept, load_owners):
        load.start()

    barrier = pltpu.get_barrier_semaphore()

    def greet(k, carry):
        o = lax.rem(me + k, ndev)
        pl.semaphore_signal(
            barrier,
            inc=1,
            device_id={"src": o // nrcv, "rcv": lax.rem(o, nrcv)},
            device_id_type=MESH,
        )
        return carry

    lax.fori_loop(1, ndev, greet, 0)

    def order(t):
        return jnp.where(t < half - 2, t + 1, jnp.where(t == half - 2, 0, half - 1))

    def at_position(h, n):
        return h * half + r * (half - 1) + n * (1 - 2 * r)

    def place(h, t):
        return at_position(h, order(t))

    tall = CHUNK + 2 * LANES
    k_ids = lax.broadcasted_iota(jnp.int32, (tall, CHUNK), 0) - LANES
    n_ids = lax.broadcasted_iota(jnp.int32, (tall, CHUNK), 1)
    band[...] = jnp.where((k_ids >= n_ids - HALF) & (k_ids <= n_ids + HALF), 1.0, 0.0).astype(bf16)

    zero = jnp.zeros((windows * local, LANES), bf16)
    outer = pl.ds(pl.multiple_of(r * (LANES + width), LANES), LANES)
    for buffer in (mag_hi, mag_lo):
        buffer[:, outer] = zero

    def turn_half(n, h):
        def turn_rows(c, carry):
            for w in range(windows):
                first = (w * 2 * tiles + h * 2 * per_half) * local
                rows = raw[n, c * windows + w].astype(f32)
                xt[pl.ds(first + c, 2 * per_half, stride=local), :] = rows
            return carry

        lax.fori_loop(0, local, turn_rows, 0, unroll=4)

    load_sent.wait()
    turn_half(0, 1 - par)

    def plane(w, tile, p):
        at = pl.multiple_of(((w * tiles + tile) * 2 + p) * local, 8)
        return xt[pl.ds(at, local), :]

    def magnitude(w, tile):
        re = plane(w, tile, 0)
        im = plane(w, tile, 1)
        m = jnp.sqrt(re * re + im * im)
        hi = m.astype(bf16)
        return hi, (m - hi.astype(f32)).astype(bf16)

    def magnitude_tile(tile):
        for w in range(windows):
            at = pl.ds(pl.multiple_of(LANES + tile * LANES, LANES), LANES)
            rows = pl.ds(w * local, local)
            mag_hi[rows, at], mag_lo[rows, at] = magnitude(w, tile)

    def magnitudes(j, carry):
        for d in range(CHUNK // LANES):
            magnitude_tile(j * (CHUNK // LANES) + d)
        return carry

    def inside(j):
        return jnp.minimum(jnp.maximum(j, 0), chunks - 1)

    def whiten(j):
        span = pl.ds(pl.multiple_of(j * CHUNK, LANES), tall)
        total = jnp.dot(mag_hi[:, span], band[...], preferred_element_type=f32)
        total = total + jnp.dot(mag_lo[:, span], band[...], preferred_element_type=f32)
        inverse = 1.0 / (total / (2 * HALF + 1) + smooth_eps)
        for w in range(windows):
            for d in range(CHUNK // LANES):
                lanes = slice(d * LANES, (d + 1) * LANES)
                part = inverse[w * local : (w + 1) * local, lanes]
                for p in range(2):
                    x = plane(w, j * (CHUNK // LANES) + d, p)
                    white[j, 2 * w + p, :, lanes] = (x * part).astype(bf16)

    partner = s + 1 - 2 * par
    beyond = s + 2 - 4 * par
    sends_far = (beyond >= 0) & (beyond < nsrc)
    back = s - 2 + 4 * par
    has_far = (back >= 0) & (back < nsrc)

    def near_copy(t, k):
        return pltpu.make_async_remote_copy(
            src_ref=white.at[place(1 - par, t), k],
            dst_ref=near.at[t, k],
            send_sem=near_send.at[t, k],
            recv_sem=near_recv.at[t, k],
            device_id={"src": partner},
            device_id_type=MESH,
        )

    def far_copy(t, k):
        return pltpu.make_async_remote_copy(
            src_ref=near.at[t, k],
            dst_ref=far.at[t, k],
            send_sem=far_send.at[t, k],
            recv_sem=far_recv.at[t, k],
            device_id={"src": beyond},
            device_id_type=MESH,
        )

    def direct_copy(u, k):
        return pltpu.make_async_remote_copy(
            src_ref=white.at[place(par, relayed + u), k],
            dst_ref=direct.at[u, k],
            send_sem=direct_send.at[u, k],
            recv_sem=direct_recv.at[u, k],
            device_id={"src": back},
            device_id_type=MESH,
        )


    def halo_copy(n):
        buffer = (mag_hi, mag_lo)[n]
        return pltpu.make_async_remote_copy(
            src_ref=edge_out.at[n],
            dst_ref=buffer.at[:, outer],
            send_sem=halo_send.at[n],
            recv_sem=halo_recv.at[n],
            device_id={"rcv": 1 - r},
            device_id_type=MESH,
        )

    def lab_copy(slot, to):
        return pltpu.make_async_remote_copy(
            src_ref=lab_out,
            dst_ref=lab_in.at[slot],
            send_sem=lab_send.at[slot],
            recv_sem=lab_recv.at[slot],
            device_id={"src": to},
            device_id_type=MESH,
        )

    label_pass = pltpu.make_async_remote_copy(
        src_ref=lab_in.at[1],
        dst_ref=lab_in.at[0],
        send_sem=lab_send.at[2],
        recv_sem=lab_recv.at[0],
        device_id={"src": s + 2},
        device_id_type=MESH,
    )

    sends_next = s + 1 < nsrc
    sends_label = (par == 0) & sends_next
    sends_second = (par == 1) & sends_next
    passes_label = (par == 0) & sends_far

    first_chunk = place(1 - par, 0)
    for d in range(-1, CHUNK // LANES + 1):
        magnitude_tile(first_chunk * (CHUNK // LANES) + d)
    whiten(first_chunk)
    pl.semaphore_wait(barrier, ndev - 1)

    def send_near(t):
        for k in range(parts):
            near_copy(t, k).start()

    send_near(0)

    load_labels.wait()
    labels = labels_ref[...]
    lab_out[...] = labels.astype(f32).astype(bf16)

    @pl.when(sends_label)
    def _():
        lab_copy(0, s + 1).start()

    @pl.when(sends_second)
    def _():
        lab_copy(1, s - 1).start()
        lab_copy(2, s + 2).start()

    load_kept.wait()
    turn_half(1, par)
    for w in range(windows):
        rows = pl.ds(w * local, local)
        edge_out[0, rows], edge_out[1, rows] = magnitude(w, (1 - r) * (tiles - 1))
    for n in range(2):
        halo_copy(n).start()

    def all_magnitudes(n, carry):
        return magnitudes(at_position(1 - par, n), carry)

    lax.fori_loop(0, half, all_magnitudes, 0)
    for n in (-1, half):
        magnitudes(inside(at_position(1 - par, n)), 0)

    def send_next(t, carry):
        whiten(place(1 - par, t))
        send_near(t)
        return carry

    lax.fori_loop(1, half - 1, send_next, 0)
    for n in range(2):
        halo_copy(n).wait_recv()
    whiten(place(1 - par, half - 1))
    send_near(half - 1)

    def keep_magnitude(t, carry):
        return magnitudes(place(par, t), carry)

    lax.fori_loop(0, half, keep_magnitude, 0)

    def keep_direct(u, carry):
        whiten(place(par, relayed + u))

        @pl.when(has_far)
        def _():
            for k in range(parts):
                direct_copy(u, k).start()

        return carry

    lax.fori_loop(0, half - relayed, keep_direct, 0)

    def keep(t, carry):
        whiten(place(par, t))
        return carry

    lax.fori_loop(0, relayed, keep, 0)

    lanes = count_out.shape[1]
    lane_ids = lax.broadcasted_iota(jnp.int32, (1, lanes), 1)
    valid = sends_next.astype(f32)

    def expand(b, counted):
        hits = jnp.where(labels == b, 1.0, 0.0).astype(f32)
        onehot[0, pl.ds(pl.multiple_of(b * local, 16), local), :] = hits.astype(bf16)
        found = jnp.sum(jnp.sum(hits, axis=0, keepdims=True), axis=1, keepdims=True)
        return counted + jnp.where(lane_ids == b, found, 0.0)

    counted = lax.fori_loop(0, nbins, expand, jnp.zeros((1, lanes), f32)) * valid
    count_out[...] = counted
    count_in[s] = counted

    def count_copy(o, slot):
        return pltpu.make_async_remote_copy(
            src_ref=count_out,
            dst_ref=count_in.at[slot],
            send_sem=count_send.at[o],
            recv_sem=count_recv.at[slot],
            device_id={"src": o},
            device_id_type=MESH,
        )

    def send_count(k, carry):
        count_copy(lax.rem(s + k, nsrc), s).start()
        return carry

    lax.fori_loop(1, nsrc, send_count, 0)

    def expand_into(which, table):
        def one(b, carry):
            onehot[which, pl.ds(pl.multiple_of(b * local, 16), local), :] = jnp.where(
                table == b, 1.0, 0.0
            ).astype(bf16)
            return carry

        lax.fori_loop(0, nbins, one, 0)

    @pl.when(par == 1)
    def _():
        lab_copy(0, s).wait_recv()
        expand_into(1, jnp.transpose(lab_in[0].astype(f32)).astype(jnp.int32))

    @pl.when(jnp.logical_not(sends_far))
    def _():
        onehot[2] = jnp.zeros((nbins * local, local), bf16)

    @pl.when(passes_label)
    def _():
        lab_copy(1, s).wait_recv()
        label_pass.start()
        expand_into(2, jnp.transpose(lab_in[1].astype(f32)).astype(jnp.int32))

    @pl.when(sends_far & (par == 1))
    def _():
        lab_copy(2, s).wait_recv()
        expand_into(2, lab_in[2].astype(f32).astype(jnp.int32))

    load_owners.wait()
    owned = owners_ref[...]
    b_rows = lax.broadcasted_iota(jnp.int32, (nbins, nbins), 0)
    b_cols = lax.broadcasted_iota(jnp.int32, (nbins, nbins), 1)
    column = jnp.sum(jnp.where(b_rows == b_cols, owned, 0).astype(f32), axis=1, keepdims=True)
    earlier = jnp.where((column.astype(jnp.int32) == owned) & (b_rows < b_cols), 1.0, 0.0)
    slots = jnp.sum(earlier.astype(f32), axis=0, keepdims=True)
    rows_row = (owned.astype(f32) * CAP + slots).astype(jnp.int32)
    lines = CAP * 4
    cols = 4 * nbins
    tiled = jnp.concatenate([rows_row] * 4, axis=1)
    batch = 16
    row_ids = lax.broadcasted_iota(jnp.int32, (batch * lines, cols), 0)
    col_group = lax.broadcasted_iota(jnp.int32, (batch * lines, cols), 1) // nbins
    same_line = lax.rem(row_ids, 4) == col_group
    row_slot = row_ids // 4

    def prepare(g, carry):
        chosen = same_line & (tiled == row_slot + g * (batch * CAP))
        at = pl.ds(pl.multiple_of(g * (batch * lines), 16), batch * lines)
        pick[at] = jnp.where(chosen, 1.0, 0.0).astype(bf16)
        return carry

    lax.fori_loop(0, ndev // batch, prepare, 0)

    group = min(nbins, 16)

    def pick_one(which, g, other, t, w, p, slot):
        rows = group * local
        picked = onehot[which, pl.ds(pl.multiple_of(g * rows, 16), rows), :]
        prod[slot + p] = jnp.dot(picked, other[t, 2 * w + p], preferred_element_type=f32)

    def picks(which, g, other, t, w, slot):
        for p in range(2):
            pick_one(which, g, other, t, w, p, slot)

    def add_products(sign, mine, g, t, slot):
        for b in range(group):
            rows = slice(b * local, (b + 1) * local)
            p_re, p_im = prod[slot, rows], prod[slot + 1, rows]
            o_re, o_im = mine[0], mine[1]
            re = (o_re * p_re + o_im * p_im).reshape(local // 8, 8, CHUNK)
            im = (o_im * p_re - o_re * p_im).reshape(local // 8, 8, CHUNK)
            acc[t, 0, g * group + b] += jnp.sum(re, axis=0)
            acc[t, 1, g * group + b] += jnp.sum(im, axis=0) * sign

    def take_own(t, w):
        for p in range(2):
            own[p] = white[place(par, t), 2 * w + p].astype(f32)

    sign_near = (1 - 2 * par).astype(f32)

    def part_copy(g, o, slot):
        return pltpu.make_async_remote_copy(
            src_ref=send_part.at[g, o],
            dst_ref=recv_part.at[g, slot],
            send_sem=part_send.at[g, o],
            recv_sem=part_recv.at[g, slot],
            device_id={"src": o // nrcv, "rcv": lax.rem(o, nrcv)},
            device_id_type=MESH,
        )

    def summed(t):
        rows = [
            jnp.sum(acc[t, q, :, :, d * LANES : (d + 1) * LANES], axis=1)
            for d in range(CHUNK // LANES)
            for q in range(2)
        ]
        return jnp.concatenate(rows, axis=0).astype(bf16)

    def route(g):
        stacked = [summed(2 * g + u) for u in range(2)]

        def some(q, carry):
            at = pl.ds(pl.multiple_of(q * (batch * lines), 16), batch * lines)
            wide = [jnp.dot(pick[at], rhs, preferred_element_type=f32) for rhs in stacked]
            for n in range(batch):
                both = [v[n * lines : (n + 1) * lines] for v in wide]
                send_part[g, q * batch + n] = jnp.concatenate(both, axis=0).astype(bf16)
            return carry

        lax.fori_loop(0, ndev // batch, some, 0)

        def send_one(k, carry):
            part_copy(g, lax.rem(me + k, ndev), me).start()
            return carry

        lax.fori_loop(1, ndev, send_one, 0)
        recv_part[g, me] = send_part[g, me]

    acc[...] = jnp.zeros(acc.shape, f32)

    def far_piece(q):
        t, w = q // windows, lax.rem(q, windows)
        for p in range(2):
            far_copy(t, 2 * w + p).wait_recv()
        take_own(t, w)

        def some(g, carry):
            picks(1 - par, g, far, t, w, 0)
            add_products(-sign_near, own, g, t, 0)
            return carry

        lax.fori_loop(0, nbins // group, some, 0)

    def relay_piece(q, carry):
        t, w = q // windows, lax.rem(q, windows)
        for p in range(2):
            near_copy(t, 2 * w + p).wait_recv()

            @pl.when(sends_far)
            def _():
                far_copy(t, 2 * w + p).start()

        take_own(t, w)

        def some(g, carry):
            picks(par, g, near, t, w, 0)
            add_products(sign_near, own, g, t, 0)
            return carry

        lax.fori_loop(0, nbins // group, some, 0)

        return carry

    lax.fori_loop(0, relayed * windows, relay_piece, 0)

    @pl.when((par == 0) & has_far)
    def _():
        lab_copy(0, s).wait_recv()
        expand_into(1, jnp.transpose(lab_in[0].astype(f32)).astype(jnp.int32))

    @pl.when(sends_far)
    def _():
        for u in range(half - relayed):
            for k in range(parts):
                direct_copy(u, k).wait_recv()

    def direct_piece(q, carry):
        t, w = q // windows, lax.rem(q, windows)
        take_own(t, w)

        @pl.when(sends_far)
        def _():
            for p in range(2):
                own_d[p] = direct[t - relayed, 2 * w + p].astype(f32)

        for p in range(2):
            near_copy(t, 2 * w + p).wait_recv()

        def some(g, carry):
            picks(par, g, near, t, w, 0)
            picks(2, g, near, t, w, 2)
            add_products(sign_near, own, g, t, 0)
            add_products(-sign_near, own_d, g, t, 2)
            return carry

        lax.fori_loop(0, nbins // group, some, 0)

        @pl.when(has_far & (t == relayed))
        def _():
            def some_far(n, inner):
                far_piece(w * relayed + n)
                return inner

            lax.fori_loop(0, relayed, some_far, 0)

        @pl.when((t == half - 2) & (w == windows - 1))
        def _():
            route(0)

        return carry

    own_d[...] = jnp.zeros(own_d.shape, f32)
    lax.fori_loop(relayed * windows, half * windows, direct_piece, 0)

    route(1)

    def take_count(k, carry):
        o = lax.rem(s + k, nsrc)
        count_copy(o, o).wait_recv()
        return carry

    lax.fori_loop(1, nsrc, take_count, 0)
    counts = jnp.sum(count_in[...], axis=0)[0:1, :nbins]
    scale = []
    for c in range(CAP):
        mine = jnp.sum(jnp.where(rows_row == me * CAP + c, counts, 0.0), axis=1, keepdims=True)
        scale.append(1.0 / jnp.sqrt(jnp.maximum(mine, 1.0)))
    for g in range(half // 2):

        def take_part(k, carry):
            o = lax.rem(me + k, ndev)
            part_copy(g, o, o).wait_recv()
            return carry

        lax.fori_loop(1, ndev, take_part, 0)
        for rr in range(nrcv):
            for pp in range(2):

                def add(z, total):
                    return total + recv_part[g, (2 * z + pp) * nrcv + rr].astype(f32)

                total = lax.fori_loop(0, nsrc // 2, add, jnp.zeros((2 * lines, LANES), f32))
                for u in range(2):
                    t = 2 * g + u
                    n = t + 1 if t < half - 2 else 0 if t == half - 2 else half - 1
                    j = pp * half + rr * (half - 1) + n * (1 - 2 * rr)
                    for c in range(CAP):
                        row = (c * nrcv * chunks + rr * chunks + j) * 4
                        value = total[u * lines + c * 4 : u * lines + c * 4 + 4]
                        out_ref[row : row + 4] = value * scale[c]

    for t in range(half):
        for k in range(parts):
            near_copy(t, k).wait_send()

    @pl.when(sends_far)
    def _():
        for t in range(relayed):
            for k in range(parts):
                far_copy(t, k).wait_send()

    @pl.when(has_far)
    def _():
        for u in range(half - relayed):
            for k in range(parts):
                direct_copy(u, k).wait_send()

    for n in range(2):
        halo_copy(n).wait_send()

    @pl.when(sends_label)
    def _():
        lab_copy(0, s + 1).wait_send()

    @pl.when(passes_label)
    def _():
        label_pass.wait_send()

    @pl.when(sends_second)
    def _():
        lab_copy(1, s - 1).wait_send()
        lab_copy(2, s + 2).wait_send()

    def end_count(k, carry):
        count_copy(lax.rem(s + k, nsrc), s).wait_send()
        return carry

    lax.fori_loop(1, nsrc, end_count, 0)

    def end_part(k, carry):
        for g in range(half // 2):
            part_copy(g, lax.rem(me + k, ndev), me).wait_send()
        return carry

    lax.fori_loop(1, ndev, end_part, 0)


def per_device(spectra, pair_bins, owners):
    local, windows, _, width = spectra.shape
    nbins = owners.shape[0]
    nsrc = lax.axis_size("src")
    nrcv = lax.axis_size("rcv")
    ndev = nsrc * nrcv
    chunks = width // CHUNK
    half = chunks // 2
    relayed = half // 2
    tiles = width // LANES
    parts = 2 * windows
    lanes = -(-nbins // 128) * 128
    group = min(nbins, 16)
    x = spectra.reshape(local * windows, 2, tiles, LANES).transpose(0, 2, 1, 3)
    x = x.reshape(local * windows, 2 * tiles, LANES)
    dims = (nsrc, nrcv, nbins, local, windows, chunks)
    bf16, f32 = jnp.bfloat16, jnp.float32
    dma = pltpu.SemaphoreType.DMA
    hbm = pl.BlockSpec(memory_space=pltpu.HBM)
    args = [
        pltpu.with_memory_space_constraint(v, pltpu.HBM) for v in (x, pair_bins, owners[None])
    ]
    out = pl.pallas_call(
        functools.partial(kernel, dims),
        out_shape=jax.ShapeDtypeStruct((CAP * nrcv * tiles * 2, LANES), f32),
        in_specs=[hbm] * 3,
        out_specs=pl.BlockSpec(memory_space=pltpu.VMEM),
        scratch_shapes=[
            pltpu.VMEM((2, local * windows, tiles, LANES), bf16),
            pltpu.VMEM((windows * 2 * tiles * local, LANES), f32),
            pltpu.VMEM((chunks, parts, local, CHUNK), bf16),
            pltpu.VMEM((half, parts, local, CHUNK), bf16),
            pltpu.VMEM((relayed, parts, local, CHUNK), bf16),
            pltpu.VMEM((half - relayed, parts, local, CHUNK), bf16),
            pltpu.VMEM((windows * local, width + 2 * LANES), bf16),
            pltpu.VMEM((windows * local, width + 2 * LANES), bf16),
            pltpu.VMEM((2, windows * local, LANES), bf16),
            pltpu.VMEM((CHUNK + 2 * LANES, CHUNK), bf16),
            pltpu.VMEM((3, nbins * local, local), bf16),
            pltpu.VMEM((2, local, CHUNK), f32),
            pltpu.VMEM((2, local, CHUNK), f32),
            pltpu.VMEM((4, group * local, CHUNK), f32),
            pltpu.VMEM((half, 2, nbins, 8, CHUNK), f32),
            pltpu.VMEM((ndev * CAP * 4, 4 * nbins), bf16),
            pltpu.VMEM((half // 2, ndev, CAP * 8, LANES), bf16),
            pltpu.VMEM((half // 2, ndev, CAP * 8, LANES), bf16),
            pltpu.VMEM((local, local), jnp.int32),
            pltpu.VMEM((1, nbins), jnp.int32),
            pltpu.VMEM((local, local), bf16),
            pltpu.VMEM((3, local, local), bf16),
            pltpu.VMEM((1, lanes), f32),
            pltpu.VMEM((nsrc, 1, lanes), f32),
            dma((4,)),
            dma((half, parts)),
            dma((half, parts)),
            dma((relayed, parts)),
            dma((relayed, parts)),
            dma((half - relayed, parts)),
            dma((half - relayed, parts)),
            dma((2,)),
            dma((2,)),
            dma((3,)),
            dma((3,)),
            dma((nsrc,)),
            dma((nsrc,)),
            dma((half // 2, ndev)),
            dma((half // 2, ndev)),
        ],
        compiler_params=pltpu.CompilerParams(
            collective_id=0, has_side_effects=True, vmem_limit_bytes=48 * 1024 * 1024
        ),
    )(*args)
    out = out.reshape(CAP, nrcv * tiles, 2, LANES).transpose(0, 2, 1, 3)
    return out.reshape(CAP, 2, nrcv * width)


def solution(mesh):
    in_specs = (P(("groups", "src"), None, None, "rcv"), P(("groups", "src"), None), P("groups"))
    out_specs = P(("groups", "src", "rcv"), None, None)
    return jax.shard_map(
        per_device, mesh=mesh, in_specs=in_specs, out_specs=out_specs, check_vma=False
    )
```

```python
import functools

import jax
import jax.numpy as jnp
from jax import lax
from jax.experimental import pallas as pl
from jax.experimental.pallas import tpu as pltpu
from jax.sharding import PartitionSpec as P

HALF = 32
CAP = 2
LANES = 128
CHUNK = 256
smooth_eps = 1e-06
MESH = pl.DeviceIdType.MESH


def kernel(
    dims,
    x_hbm,
    lab_hbm,
    owners_hbm,
    out_ref,
    raw,
    xt,
    white,
    near,
    far,
    direct,
    mag_hi,
    mag_lo,
    edge_out,
    band,
    onehot,
    own,
    own_d,
    prod,
    acc,
    pick,
    send_part,
    recv_part,
    labels_ref,
    owners_ref,
    lab_out,
    lab_in,
    count_out,
    count_in,
    load_sems,
    near_send,
    near_recv,
    far_send,
    far_recv,
    direct_send,
    direct_recv,
    halo_send,
    halo_recv,
    lab_send,
    lab_recv,
    count_send,
    count_recv,
    part_send,
    part_recv,
):
    nsrc, nrcv, nbins, local, windows, chunks = dims
    half = chunks // 2
    relayed = half // 2
    parts = 2 * windows
    width = chunks * CHUNK
    tiles = width // LANES
    per_half = tiles // 2
    ndev = nsrc * nrcv
    steps = 5 if (ndev - 1) % 5 == 0 else 1
    s = lax.axis_index("src")
    r = lax.axis_index("rcv")
    me = s * nrcv + r
    par = lax.rem(s, 2)
    f32 = jnp.float32
    bf16 = jnp.bfloat16

    def load_half(n, h):
        rows = pl.ds(pl.multiple_of(h * 2 * per_half, 16), 2 * per_half)
        return pltpu.make_async_copy(x_hbm.at[:, rows], raw.at[n], load_sems.at[n])

    load_sent = load_half(0, 1 - par)
    load_kept = load_half(1, par)
    load_labels = pltpu.make_async_copy(lab_hbm, labels_ref, load_sems.at[2])
    load_owners = pltpu.make_async_copy(owners_hbm, owners_ref, load_sems.at[3])
    for load in (load_sent, load_labels, load_kept, load_owners):
        load.start()

    barrier = pltpu.get_barrier_semaphore()

    def greet(k, carry):
        o = lax.rem(me + k, ndev)
        pl.semaphore_signal(
            barrier,
            inc=1,
            device_id={"src": o // nrcv, "rcv": lax.rem(o, nrcv)},
            device_id_type=MESH,
        )
        return carry

    lax.fori_loop(1, ndev, greet, 0)

    def order(t):
        return jnp.where(t < half - 2, t + 1, jnp.where(t == half - 2, 0, half - 1))

    def at_position(h, n):
        return h * half + r * (half - 1) + n * (1 - 2 * r)

    def place(h, t):
        return at_position(h, order(t))

    tall = CHUNK + 2 * LANES
    k_ids = lax.broadcasted_iota(jnp.int32, (tall, CHUNK), 0) - LANES
    n_ids = lax.broadcasted_iota(jnp.int32, (tall, CHUNK), 1)
    band[...] = jnp.where((k_ids >= n_ids - HALF) & (k_ids <= n_ids + HALF), 1.0, 0.0).astype(bf16)

    zero = jnp.zeros((windows * local, LANES), bf16)
    outer = pl.ds(pl.multiple_of(r * (LANES + width), LANES), LANES)
    for buffer in (mag_hi, mag_lo):
        buffer[:, outer] = zero

    def turn_half(n, h):
        def turn_rows(c, carry):
            for w in range(windows):
                first = (w * 2 * tiles + h * 2 * per_half) * local
                rows = raw[n, c * windows + w].astype(f32)
                xt[pl.ds(first + c, 2 * per_half, stride=local), :] = rows
            return carry

        lax.fori_loop(0, local, turn_rows, 0, unroll=4)

    load_sent.wait()
    turn_half(0, 1 - par)

    def plane(w, tile, p):
        at = pl.multiple_of(((w * tiles + tile) * 2 + p) * local, 8)
        return xt[pl.ds(at, local), :]

    def magnitude(w, tile):
        re = plane(w, tile, 0)
        im = plane(w, tile, 1)
        m = jnp.sqrt(re * re + im * im)
        hi = m.astype(bf16)
        return hi, (m - hi.astype(f32)).astype(bf16)

    def magnitude_tile(tile):
        for w in range(windows):
            at = pl.ds(pl.multiple_of(LANES + tile * LANES, LANES), LANES)
            rows = pl.ds(w * local, local)
            mag_hi[rows, at], mag_lo[rows, at] = magnitude(w, tile)

    def magnitudes(j, carry):
        for d in range(CHUNK // LANES):
            magnitude_tile(j * (CHUNK // LANES) + d)
        return carry

    def inside(j):
        return jnp.minimum(jnp.maximum(j, 0), chunks - 1)

    def whiten(j):
        span = pl.ds(pl.multiple_of(j * CHUNK, LANES), tall)
        total = jnp.dot(mag_hi[:, span], band[...], preferred_element_type=f32)
        total = total + jnp.dot(mag_lo[:, span], band[...], preferred_element_type=f32)
        inverse = 1.0 / (total / (2 * HALF + 1) + smooth_eps)
        for w in range(windows):
            for d in range(CHUNK // LANES):
                lanes = slice(d * LANES, (d + 1) * LANES)
                part = inverse[w * local : (w + 1) * local, lanes]
                for p in range(2):
                    x = plane(w, j * (CHUNK // LANES) + d, p)
                    white[j, 2 * w + p, :, lanes] = (x * part).astype(bf16)

    partner = s + 1 - 2 * par
    beyond = s + 2 - 4 * par
    sends_far = (beyond >= 0) & (beyond < nsrc)
    back = s - 2 + 4 * par
    has_far = (back >= 0) & (back < nsrc)

    def near_copy(t, k):
        return pltpu.make_async_remote_copy(
            src_ref=white.at[place(1 - par, t), k],
            dst_ref=near.at[t, k],
            send_sem=near_send.at[t, k],
            recv_sem=near_recv.at[t, k],
            device_id={"src": partner},
            device_id_type=MESH,
        )

    def far_copy(t, k):
        return pltpu.make_async_remote_copy(
            src_ref=near.at[t, k],
            dst_ref=far.at[t, k],
            send_sem=far_send.at[t, k],
            recv_sem=far_recv.at[t, k],
            device_id={"src": beyond},
            device_id_type=MESH,
        )

    def direct_copy(u, k):
        return pltpu.make_async_remote_copy(
            src_ref=white.at[place(par, relayed + u), k],
            dst_ref=direct.at[u, k],
            send_sem=direct_send.at[u, k],
            recv_sem=direct_recv.at[u, k],
            device_id={"src": back},
            device_id_type=MESH,
        )


    def halo_copy(n):
        buffer = (mag_hi, mag_lo)[n]
        return pltpu.make_async_remote_copy(
            src_ref=edge_out.at[n],
            dst_ref=buffer.at[:, outer],
            send_sem=halo_send.at[n],
            recv_sem=halo_recv.at[n],
            device_id={"rcv": 1 - r},
            device_id_type=MESH,
        )

    def lab_copy(slot, to):
        return pltpu.make_async_remote_copy(
            src_ref=lab_out,
            dst_ref=lab_in.at[slot],
            send_sem=lab_send.at[slot],
            recv_sem=lab_recv.at[slot],
            device_id={"src": to},
            device_id_type=MESH,
        )

    label_pass = pltpu.make_async_remote_copy(
        src_ref=lab_in.at[1],
        dst_ref=lab_in.at[0],
        send_sem=lab_send.at[2],
        recv_sem=lab_recv.at[0],
        device_id={"src": s + 2},
        device_id_type=MESH,
    )

    sends_next = s + 1 < nsrc
    sends_label = (par == 0) & sends_next
    sends_second = (par == 1) & sends_next
    passes_label = (par == 0) & sends_far

    first_chunk = place(1 - par, 0)
    for d in range(-1, CHUNK // LANES + 1):
        magnitude_tile(first_chunk * (CHUNK // LANES) + d)
    whiten(first_chunk)
    load_labels.wait()
    labels = labels_ref[...]
    lab_out[...] = labels.astype(f32).astype(bf16)
    pl.semaphore_wait(barrier, ndev - 1)

    @pl.when(sends_label)
    def _():
        lab_copy(0, s + 1).start()

    @pl.when(sends_second)
    def _():
        lab_copy(1, s - 1).start()
        lab_copy(2, s + 2).start()

    def send_near(t):
        for k in range(parts):
            near_copy(t, k).start()

    send_near(0)


    load_kept.wait()
    turn_half(1, par)
    for w in range(windows):
        rows = pl.ds(w * local, local)
        edge_out[0, rows], edge_out[1, rows] = magnitude(w, (1 - r) * (tiles - 1))
    for n in range(2):
        halo_copy(n).start()

    def all_magnitudes(n, carry):
        return magnitudes(at_position(1 - par, n), carry)

    lax.fori_loop(0, half, all_magnitudes, 0)
    for n in (-1, half):
        magnitudes(inside(at_position(1 - par, n)), 0)

    def send_next(t, carry):
        whiten(place(1 - par, t))
        send_near(t)
        return carry

    lax.fori_loop(1, half - 1, send_next, 0)
    for n in range(2):
        halo_copy(n).wait_recv()
    whiten(place(1 - par, half - 1))
    send_near(half - 1)

    def keep_magnitude(t, carry):
        return magnitudes(place(par, t), carry)

    lax.fori_loop(0, half, keep_magnitude, 0)

    def keep_direct(u, carry):
        whiten(place(par, relayed + u))

        @pl.when(has_far)
        def _():
            for k in range(parts):
                direct_copy(u, k).start()

        return carry

    lax.fori_loop(0, half - relayed, keep_direct, 0)

    def keep(t, carry):
        whiten(place(par, t))
        return carry

    lax.fori_loop(0, relayed, keep, 0)

    lanes = count_out.shape[1]
    lane_ids = lax.broadcasted_iota(jnp.int32, (1, lanes), 1)
    valid = sends_next.astype(f32)

    def expand(b, counted):
        hits = jnp.where(labels == b, 1.0, 0.0).astype(f32)
        onehot[0, pl.ds(pl.multiple_of(b * local, 16), local), :] = hits.astype(bf16)
        found = jnp.sum(jnp.sum(hits, axis=0, keepdims=True), axis=1, keepdims=True)
        return counted + jnp.where(lane_ids == b, found, 0.0)

    counted = lax.fori_loop(0, nbins, expand, jnp.zeros((1, lanes), f32)) * valid
    count_out[...] = counted
    count_in[s] = counted

    def count_copy(o, slot):
        return pltpu.make_async_remote_copy(
            src_ref=count_out,
            dst_ref=count_in.at[slot],
            send_sem=count_send.at[o],
            recv_sem=count_recv.at[slot],
            device_id={"src": o},
            device_id_type=MESH,
        )

    def send_count(k, carry):
        count_copy(lax.rem(s + k, nsrc), s).start()
        return carry

    lax.fori_loop(1, nsrc, send_count, 0)

    def expand_into(which, table):
        def one(b, carry):
            onehot[which, pl.ds(pl.multiple_of(b * local, 16), local), :] = jnp.where(
                table == b, 1.0, 0.0
            ).astype(bf16)
            return carry

        lax.fori_loop(0, nbins, one, 0)

    @pl.when(par == 1)
    def _():
        lab_copy(0, s).wait_recv()
        expand_into(1, jnp.transpose(lab_in[0].astype(f32)).astype(jnp.int32))

    @pl.when(jnp.logical_not(sends_far))
    def _():
        onehot[2] = jnp.zeros((nbins * local, local), bf16)

    @pl.when(passes_label)
    def _():
        lab_copy(1, s).wait_recv()
        label_pass.start()
        expand_into(2, jnp.transpose(lab_in[1].astype(f32)).astype(jnp.int32))

    @pl.when(sends_far & (par == 1))
    def _():
        lab_copy(2, s).wait_recv()
        expand_into(2, lab_in[2].astype(f32).astype(jnp.int32))

    load_owners.wait()
    owned = owners_ref[...]
    b_rows = lax.broadcasted_iota(jnp.int32, (nbins, nbins), 0)
    b_cols = lax.broadcasted_iota(jnp.int32, (nbins, nbins), 1)
    column = jnp.sum(jnp.where(b_rows == b_cols, owned, 0).astype(f32), axis=1, keepdims=True)
    earlier = jnp.where((column.astype(jnp.int32) == owned) & (b_rows < b_cols), 1.0, 0.0)
    slots = jnp.sum(earlier.astype(f32), axis=0, keepdims=True)
    rows_row = (owned.astype(f32) * CAP + slots).astype(jnp.int32)
    lines = CAP * 4
    cols = 4 * nbins
    tiled = jnp.concatenate([rows_row] * 4, axis=1)
    batch = 16
    row_ids = lax.broadcasted_iota(jnp.int32, (batch * lines, cols), 0)
    col_group = lax.broadcasted_iota(jnp.int32, (batch * lines, cols), 1) // nbins
    same_line = lax.rem(row_ids, 4) == col_group
    row_slot = row_ids // 4

    def prepare(g, carry):
        chosen = same_line & (tiled == row_slot + g * (batch * CAP))
        at = pl.ds(pl.multiple_of(g * (batch * lines), 16), batch * lines)
        pick[at] = jnp.where(chosen, 1.0, 0.0).astype(bf16)
        return carry

    lax.fori_loop(0, ndev // batch, prepare, 0)

    group = min(nbins, 16)

    def pick_one(which, g, other, t, w, p, slot):
        rows = group * local
        picked = onehot[which, pl.ds(pl.multiple_of(g * rows, 16), rows), :]
        prod[slot + p] = jnp.dot(picked, other[t, 2 * w + p], preferred_element_type=f32)

    def picks(which, g, other, t, w, slot):
        for p in range(2):
            pick_one(which, g, other, t, w, p, slot)

    def add_products(sign, mine, g, t, slot):
        for b in range(group):
            rows = slice(b * local, (b + 1) * local)
            p_re, p_im = prod[slot, rows], prod[slot + 1, rows]
            o_re, o_im = mine[0], mine[1]
            re = (o_re * p_re + o_im * p_im).reshape(local // 8, 8, CHUNK)
            im = (o_im * p_re - o_re * p_im).reshape(local // 8, 8, CHUNK)
            acc[t, 0, g * group + b] += jnp.sum(re, axis=0)
            acc[t, 1, g * group + b] += jnp.sum(im, axis=0) * sign

    def take_own(t, w):
        for p in range(2):
            own[p] = white[place(par, t), 2 * w + p].astype(f32)

    sign_near = (1 - 2 * par).astype(f32)

    def part_copy(g, o, slot):
        return pltpu.make_async_remote_copy(
            src_ref=send_part.at[g, o],
            dst_ref=recv_part.at[g, slot],
            send_sem=part_send.at[g, o],
            recv_sem=part_recv.at[g, slot],
            device_id={"src": o // nrcv, "rcv": lax.rem(o, nrcv)},
            device_id_type=MESH,
        )

    def summed(t):
        rows = [
            jnp.sum(acc[t, q, :, :, d * LANES : (d + 1) * LANES], axis=1)
            for d in range(CHUNK // LANES)
            for q in range(2)
        ]
        return jnp.concatenate(rows, axis=0).astype(bf16)

    def route(g):
        stacked = [summed(2 * g + u) for u in range(2)]

        def some(q, carry):
            at = pl.ds(pl.multiple_of(q * (batch * lines), 16), batch * lines)
            wide = [jnp.dot(pick[at], rhs, preferred_element_type=f32) for rhs in stacked]
            for n in range(batch):
                both = [v[n * lines : (n + 1) * lines] for v in wide]
                send_part[g, q * batch + n] = jnp.concatenate(both, axis=0).astype(bf16)
            return carry

        lax.fori_loop(0, ndev // batch, some, 0)

        def send_one(k, carry):
            part_copy(g, lax.rem(me + k, ndev), me).start()
            return carry

        lax.fori_loop(1, ndev, send_one, 0, unroll=steps)
        recv_part[g, me] = send_part[g, me]

    acc[...] = jnp.zeros(acc.shape, f32)

    def far_piece(q):
        t, w = q // windows, lax.rem(q, windows)
        for p in range(2):
            far_copy(t, 2 * w + p).wait_recv()
        take_own(t, w)

        def some(g, carry):
            picks(1 - par, g, far, t, w, 0)
            add_products(-sign_near, own, g, t, 0)
            return carry

        lax.fori_loop(0, nbins // group, some, 0)

    def relay_piece(q, carry):
        t, w = q // windows, lax.rem(q, windows)
        for p in range(2):
            near_copy(t, 2 * w + p).wait_recv()

            @pl.when(sends_far)
            def _():
                far_copy(t, 2 * w + p).start()

        take_own(t, w)

        def some(g, carry):
            picks(par, g, near, t, w, 0)
            add_products(sign_near, own, g, t, 0)
            return carry

        lax.fori_loop(0, nbins // group, some, 0)

        return carry

    lax.fori_loop(0, relayed * windows, relay_piece, 0)

    @pl.when((par == 0) & has_far)
    def _():
        lab_copy(0, s).wait_recv()
        expand_into(1, jnp.transpose(lab_in[0].astype(f32)).astype(jnp.int32))

    @pl.when(sends_far)
    def _():
        for u in range(half - relayed):
            for k in range(parts):
                direct_copy(u, k).wait_recv()

    def direct_piece(q, carry):
        t, w = q // windows, lax.rem(q, windows)
        take_own(t, w)

        @pl.when(sends_far)
        def _():
            for p in range(2):
                own_d[p] = direct[t - relayed, 2 * w + p].astype(f32)

        for p in range(2):
            near_copy(t, 2 * w + p).wait_recv()

        def some(g, carry):
            picks(par, g, near, t, w, 0)
            picks(2, g, near, t, w, 2)
            add_products(sign_near, own, g, t, 0)
            add_products(-sign_near, own_d, g, t, 2)
            return carry

        lax.fori_loop(0, nbins // group, some, 0)

        @pl.when(has_far & (t == relayed))
        def _():
            def some_far(n, inner):
                far_piece(w * relayed + n)
                return inner

            lax.fori_loop(0, relayed, some_far, 0)

        @pl.when((t == half - 2) & (w == windows - 1))
        def _():
            route(0)

        return carry

    own_d[...] = jnp.zeros(own_d.shape, f32)
    lax.fori_loop(relayed * windows, half * windows, direct_piece, 0)

    route(1)

    def take_count(k, carry):
        o = lax.rem(s + k, nsrc)
        count_copy(o, o).wait_recv()
        return carry

    lax.fori_loop(1, nsrc, take_count, 0)
    counts = jnp.sum(count_in[...], axis=0)[0:1, :nbins]
    scale = []
    for c in range(CAP):
        mine = jnp.sum(jnp.where(rows_row == me * CAP + c, counts, 0.0), axis=1, keepdims=True)
        scale.append(1.0 / jnp.sqrt(jnp.maximum(mine, 1.0)))
    for g in range(half // 2):

        def take_part(k, carry):
            o = lax.rem(me + k, ndev)
            part_copy(g, o, o).wait_recv()
            return carry

        lax.fori_loop(1, ndev, take_part, 0, unroll=steps)
        for rr in range(nrcv):
            for pp in range(2):

                def add(z, total):
                    return total + recv_part[g, (2 * z + pp) * nrcv + rr].astype(f32)

                total = jnp.zeros((2 * lines, LANES), f32)
                total = lax.fori_loop(0, nsrc // 2, add, total, unroll=4)
                for u in range(2):
                    t = 2 * g + u
                    n = t + 1 if t < half - 2 else 0 if t == half - 2 else half - 1
                    j = pp * half + rr * (half - 1) + n * (1 - 2 * rr)
                    for c in range(CAP):
                        row = (c * nrcv * chunks + rr * chunks + j) * 4
                        value = total[u * lines + c * 4 : u * lines + c * 4 + 4]
                        out_ref[row : row + 4] = value * scale[c]

    for t in range(half):
        for k in range(parts):
            near_copy(t, k).wait_send()

    @pl.when(sends_far)
    def _():
        for t in range(relayed):
            for k in range(parts):
                far_copy(t, k).wait_send()

    @pl.when(has_far)
    def _():
        for u in range(half - relayed):
            for k in range(parts):
                direct_copy(u, k).wait_send()

    for n in range(2):
        halo_copy(n).wait_send()

    @pl.when(sends_label)
    def _():
        lab_copy(0, s + 1).wait_send()

    @pl.when(passes_label)
    def _():
        label_pass.wait_send()

    @pl.when(sends_second)
    def _():
        lab_copy(1, s - 1).wait_send()
        lab_copy(2, s + 2).wait_send()

    def end_count(k, carry):
        count_copy(lax.rem(s + k, nsrc), s).wait_send()
        return carry

    lax.fori_loop(1, nsrc, end_count, 0)

    def end_part(k, carry):
        for g in range(half // 2):
            part_copy(g, lax.rem(me + k, ndev), me).wait_send()
        return carry

    lax.fori_loop(1, ndev, end_part, 0, unroll=steps)


def per_device(spectra, pair_bins, owners):
    local, windows, _, width = spectra.shape
    nbins = owners.shape[0]
    nsrc = lax.axis_size("src")
    nrcv = lax.axis_size("rcv")
    ndev = nsrc * nrcv
    chunks = width // CHUNK
    half = chunks // 2
    relayed = half // 2
    tiles = width // LANES
    parts = 2 * windows
    lanes = -(-nbins // 128) * 128
    group = min(nbins, 16)
    x = spectra.reshape(local * windows, 2, tiles, LANES).transpose(0, 2, 1, 3)
    x = x.reshape(local * windows, 2 * tiles, LANES)
    dims = (nsrc, nrcv, nbins, local, windows, chunks)
    bf16, f32 = jnp.bfloat16, jnp.float32
    dma = pltpu.SemaphoreType.DMA
    hbm = pl.BlockSpec(memory_space=pltpu.HBM)
    args = [
        pltpu.with_memory_space_constraint(v, pltpu.HBM) for v in (x, pair_bins, owners[None])
    ]
    out = pl.pallas_call(
        functools.partial(kernel, dims),
        out_shape=jax.ShapeDtypeStruct((CAP * nrcv * tiles * 2, LANES), f32),
        in_specs=[hbm] * 3,
        out_specs=pl.BlockSpec(memory_space=pltpu.VMEM),
        scratch_shapes=[
            pltpu.VMEM((2, local * windows, tiles, LANES), bf16),
            pltpu.VMEM((windows * 2 * tiles * local, LANES), f32),
            pltpu.VMEM((chunks, parts, local, CHUNK), bf16),
            pltpu.VMEM((half, parts, local, CHUNK), bf16),
            pltpu.VMEM((relayed, parts, local, CHUNK), bf16),
            pltpu.VMEM((half - relayed, parts, local, CHUNK), bf16),
            pltpu.VMEM((windows * local, width + 2 * LANES), bf16),
            pltpu.VMEM((windows * local, width + 2 * LANES), bf16),
            pltpu.VMEM((2, windows * local, LANES), bf16),
            pltpu.VMEM((CHUNK + 2 * LANES, CHUNK), bf16),
            pltpu.VMEM((3, nbins * local, local), bf16),
            pltpu.VMEM((2, local, CHUNK), f32),
            pltpu.VMEM((2, local, CHUNK), f32),
            pltpu.VMEM((4, group * local, CHUNK), f32),
            pltpu.VMEM((half, 2, nbins, 8, CHUNK), f32),
            pltpu.VMEM((ndev * CAP * 4, 4 * nbins), bf16),
            pltpu.VMEM((half // 2, ndev, CAP * 8, LANES), bf16),
            pltpu.VMEM((half // 2, ndev, CAP * 8, LANES), bf16),
            pltpu.VMEM((local, local), jnp.int32),
            pltpu.VMEM((1, nbins), jnp.int32),
            pltpu.VMEM((local, local), bf16),
            pltpu.VMEM((3, local, local), bf16),
            pltpu.VMEM((1, lanes), f32),
            pltpu.VMEM((nsrc, 1, lanes), f32),
            dma((4,)),
            dma((half, parts)),
            dma((half, parts)),
            dma((relayed, parts)),
            dma((relayed, parts)),
            dma((half - relayed, parts)),
            dma((half - relayed, parts)),
            dma((2,)),
            dma((2,)),
            dma((3,)),
            dma((3,)),
            dma((nsrc,)),
            dma((nsrc,)),
            dma((half // 2, ndev)),
            dma((half // 2, ndev)),
        ],
        compiler_params=pltpu.CompilerParams(
            collective_id=0, has_side_effects=True, vmem_limit_bytes=48 * 1024 * 1024
        ),
    )(*args)
    out = out.reshape(CAP, nrcv * tiles, 2, LANES).transpose(0, 2, 1, 3)
    return out.reshape(CAP, 2, nrcv * width)


def solution(mesh):
    in_specs = (P(("groups", "src"), None, None, "rcv"), P(("groups", "src"), None), P("groups"))
    out_specs = P(("groups", "src", "rcv"), None, None)
    return jax.shard_map(
        per_device, mesh=mesh, in_specs=in_specs, out_specs=out_specs, check_vma=False
    )
```

```python
import functools

import jax
import jax.numpy as jnp
from jax import lax
from jax.experimental import pallas as pl
from jax.experimental.pallas import tpu as pltpu
from jax.sharding import PartitionSpec as P

HALF = 32
CAP = 2
LANES = 128
CHUNK = 256
smooth_eps = 1e-06
MESH = pl.DeviceIdType.MESH


def kernel(
    dims,
    x_hbm,
    lab_hbm,
    owners_hbm,
    out_ref,
    raw,
    xt,
    white,
    near,
    far,
    direct,
    mag_hi,
    mag_lo,
    edge_out,
    band,
    onehot,
    own,
    own_d,
    prod,
    acc,
    pick,
    send_part,
    recv_part,
    labels_ref,
    owners_ref,
    lab_out,
    lab_in,
    count_out,
    count_in,
    load_sems,
    near_send,
    near_recv,
    far_send,
    far_recv,
    direct_send,
    direct_recv,
    halo_send,
    halo_recv,
    lab_send,
    lab_recv,
    count_send,
    count_recv,
    part_send,
    part_recv,
):
    nsrc, nrcv, nbins, local, windows, chunks = dims
    half = chunks // 2
    relayed = half // 2
    parts = 2 * windows
    width = chunks * CHUNK
    tiles = width // LANES
    per_half = tiles // 2
    ndev = nsrc * nrcv
    steps = ndev - 1 if ndev <= 16 else 1
    s = lax.axis_index("src")
    r = lax.axis_index("rcv")
    me = s * nrcv + r
    par = lax.rem(s, 2)
    f32 = jnp.float32
    bf16 = jnp.bfloat16

    def load_half(n, h):
        rows = pl.ds(pl.multiple_of(h * 2 * per_half, 16), 2 * per_half)
        return pltpu.make_async_copy(x_hbm.at[:, rows], raw.at[n], load_sems.at[n])

    load_sent = load_half(0, 1 - par)
    load_kept = load_half(1, par)
    load_labels = pltpu.make_async_copy(lab_hbm, labels_ref, load_sems.at[2])
    load_owners = pltpu.make_async_copy(owners_hbm, owners_ref, load_sems.at[3])
    for load in (load_sent, load_labels, load_kept, load_owners):
        load.start()

    barrier = pltpu.get_barrier_semaphore()

    def greet(k, carry):
        o = lax.rem(me + k, ndev)
        pl.semaphore_signal(
            barrier,
            inc=1,
            device_id={"src": o // nrcv, "rcv": lax.rem(o, nrcv)},
            device_id_type=MESH,
        )
        return carry

    lax.fori_loop(1, ndev, greet, 0, unroll=steps)

    def order(t):
        return jnp.where(t < half - 2, t + 1, jnp.where(t == half - 2, 0, half - 1))

    def at_position(h, n):
        return h * half + r * (half - 1) + n * (1 - 2 * r)

    def place(h, t):
        return at_position(h, order(t))

    tall = CHUNK + 2 * LANES
    k_ids = lax.broadcasted_iota(jnp.int32, (tall, CHUNK), 0) - LANES
    n_ids = lax.broadcasted_iota(jnp.int32, (tall, CHUNK), 1)
    band[...] = jnp.where((k_ids >= n_ids - HALF) & (k_ids <= n_ids + HALF), 1.0, 0.0).astype(bf16)

    zero = jnp.zeros((windows * local, LANES), bf16)
    outer = pl.ds(pl.multiple_of(r * (LANES + width), LANES), LANES)
    for buffer in (mag_hi, mag_lo):
        buffer[:, outer] = zero

    def turn_half(n, h):
        def turn_rows(c, carry):
            for w in range(windows):
                first = (w * 2 * tiles + h * 2 * per_half) * local
                rows = raw[n, c * windows + w].astype(f32)
                xt[pl.ds(first + c, 2 * per_half, stride=local), :] = rows
            return carry

        lax.fori_loop(0, local, turn_rows, 0, unroll=8)

    load_sent.wait()
    turn_half(0, 1 - par)

    def plane(w, tile, p):
        at = pl.multiple_of(((w * tiles + tile) * 2 + p) * local, 8)
        return xt[pl.ds(at, local), :]

    def magnitude(w, tile):
        re = plane(w, tile, 0)
        im = plane(w, tile, 1)
        m = jnp.sqrt(re * re + im * im)
        hi = m.astype(bf16)
        return hi, (m - hi.astype(f32)).astype(bf16)

    def magnitude_tile(tile):
        for w in range(windows):
            at = pl.ds(pl.multiple_of(LANES + tile * LANES, LANES), LANES)
            rows = pl.ds(w * local, local)
            mag_hi[rows, at], mag_lo[rows, at] = magnitude(w, tile)

    def magnitudes(j, carry):
        for d in range(CHUNK // LANES):
            magnitude_tile(j * (CHUNK // LANES) + d)
        return carry

    def inside(j):
        return jnp.minimum(jnp.maximum(j, 0), chunks - 1)

    def whiten(j):
        span = pl.ds(pl.multiple_of(j * CHUNK, LANES), tall)
        total = jnp.dot(mag_hi[:, span], band[...], preferred_element_type=f32)
        total = total + jnp.dot(mag_lo[:, span], band[...], preferred_element_type=f32)
        inverse = 1.0 / (total / (2 * HALF + 1) + smooth_eps)
        for w in range(windows):
            for d in range(CHUNK // LANES):
                lanes = slice(d * LANES, (d + 1) * LANES)
                part = inverse[w * local : (w + 1) * local, lanes]
                for p in range(2):
                    x = plane(w, j * (CHUNK // LANES) + d, p)
                    white[j, 2 * w + p, :, lanes] = (x * part).astype(bf16)

    partner = s + 1 - 2 * par
    beyond = s + 2 - 4 * par
    sends_far = (beyond >= 0) & (beyond < nsrc)
    back = s - 2 + 4 * par
    has_far = (back >= 0) & (back < nsrc)

    def near_copy(t, k):
        return pltpu.make_async_remote_copy(
            src_ref=white.at[place(1 - par, t), k],
            dst_ref=near.at[t, k],
            send_sem=near_send.at[t, k],
            recv_sem=near_recv.at[t, k],
            device_id={"src": partner},
            device_id_type=MESH,
        )

    def far_copy(t, k):
        return pltpu.make_async_remote_copy(
            src_ref=near.at[t, k],
            dst_ref=far.at[t, k],
            send_sem=far_send.at[t, k],
            recv_sem=far_recv.at[t, k],
            device_id={"src": beyond},
            device_id_type=MESH,
        )

    def direct_copy(u, k):
        return pltpu.make_async_remote_copy(
            src_ref=white.at[place(par, relayed + u), k],
            dst_ref=direct.at[u, k],
            send_sem=direct_send.at[u, k],
            recv_sem=direct_recv.at[u, k],
            device_id={"src": back},
            device_id_type=MESH,
        )


    def halo_copy(n):
        buffer = (mag_hi, mag_lo)[n]
        return pltpu.make_async_remote_copy(
            src_ref=edge_out.at[n],
            dst_ref=buffer.at[:, outer],
            send_sem=halo_send.at[n],
            recv_sem=halo_recv.at[n],
            device_id={"rcv": 1 - r},
            device_id_type=MESH,
        )

    def lab_copy(slot, to):
        return pltpu.make_async_remote_copy(
            src_ref=lab_out,
            dst_ref=lab_in.at[slot],
            send_sem=lab_send.at[slot],
            recv_sem=lab_recv.at[slot],
            device_id={"src": to},
            device_id_type=MESH,
        )

    label_pass = pltpu.make_async_remote_copy(
        src_ref=lab_in.at[1],
        dst_ref=lab_in.at[0],
        send_sem=lab_send.at[2],
        recv_sem=lab_recv.at[0],
        device_id={"src": s + 2},
        device_id_type=MESH,
    )

    sends_next = s + 1 < nsrc
    sends_label = (par == 0) & sends_next
    sends_second = (par == 1) & sends_next
    passes_label = (par == 0) & sends_far

    first_chunk = place(1 - par, 0)
    for d in range(-1, CHUNK // LANES + 1):
        magnitude_tile(first_chunk * (CHUNK // LANES) + d)
    whiten(first_chunk)
    load_labels.wait()
    labels = labels_ref[...]
    lab_out[...] = labels.astype(f32).astype(bf16)
    pl.semaphore_wait(barrier, ndev - 1)

    @pl.when(sends_label)
    def _():
        lab_copy(0, s + 1).start()

    @pl.when(sends_second)
    def _():
        lab_copy(1, s - 1).start()
        lab_copy(2, s + 2).start()

    def send_near(t):
        for k in range(parts):
            near_copy(t, k).start()

    send_near(0)


    load_kept.wait()
    turn_half(1, par)
    for w in range(windows):
        rows = pl.ds(w * local, local)
        edge_out[0, rows], edge_out[1, rows] = magnitude(w, (1 - r) * (tiles - 1))
    for n in range(2):
        halo_copy(n).start()

    def all_magnitudes(n, carry):
        return magnitudes(at_position(1 - par, n), carry)

    lax.fori_loop(0, half, all_magnitudes, 0)
    for n in (-1, half):
        magnitudes(inside(at_position(1 - par, n)), 0)

    def send_next(t, carry):
        whiten(place(1 - par, t))
        send_near(t)
        return carry

    lax.fori_loop(1, half - 1, send_next, 0)
    for n in range(2):
        halo_copy(n).wait_recv()
    whiten(place(1 - par, half - 1))
    send_near(half - 1)

    def keep_magnitude(t, carry):
        return magnitudes(place(par, t), carry)

    lax.fori_loop(0, half, keep_magnitude, 0)

    def keep_direct(u, carry):
        whiten(place(par, relayed + u))

        @pl.when(has_far)
        def _():
            for k in range(parts):
                direct_copy(u, k).start()

        return carry

    lax.fori_loop(0, half - relayed, keep_direct, 0)

    def keep(t, carry):
        whiten(place(par, t))
        return carry

    lax.fori_loop(0, relayed, keep, 0)

    lanes = count_out.shape[1]
    lane_ids = lax.broadcasted_iota(jnp.int32, (1, lanes), 1)
    valid = sends_next.astype(f32)

    def expand(b, counted):
        hits = jnp.where(labels == b, 1.0, 0.0).astype(f32)
        onehot[0, pl.ds(pl.multiple_of(b * local, 16), local), :] = hits.astype(bf16)
        found = jnp.sum(jnp.sum(hits, axis=0, keepdims=True), axis=1, keepdims=True)
        return counted + jnp.where(lane_ids == b, found, 0.0)

    counted = lax.fori_loop(0, nbins, expand, jnp.zeros((1, lanes), f32)) * valid
    count_out[...] = counted
    count_in[s] = counted

    def count_copy(o, slot):
        return pltpu.make_async_remote_copy(
            src_ref=count_out,
            dst_ref=count_in.at[slot],
            send_sem=count_send.at[o],
            recv_sem=count_recv.at[slot],
            device_id={"src": o},
            device_id_type=MESH,
        )

    def send_count(k, carry):
        count_copy(lax.rem(s + k, nsrc), s).start()
        return carry

    lax.fori_loop(1, nsrc, send_count, 0)

    def expand_into(which, table):
        def one(b, carry):
            onehot[which, pl.ds(pl.multiple_of(b * local, 16), local), :] = jnp.where(
                table == b, 1.0, 0.0
            ).astype(bf16)
            return carry

        lax.fori_loop(0, nbins, one, 0)

    @pl.when(par == 1)
    def _():
        lab_copy(0, s).wait_recv()
        expand_into(1, jnp.transpose(lab_in[0].astype(f32)).astype(jnp.int32))

    @pl.when(jnp.logical_not(sends_far))
    def _():
        onehot[2] = jnp.zeros((nbins * local, local), bf16)

    @pl.when(passes_label)
    def _():
        lab_copy(1, s).wait_recv()
        label_pass.start()
        expand_into(2, jnp.transpose(lab_in[1].astype(f32)).astype(jnp.int32))

    @pl.when(sends_far & (par == 1))
    def _():
        lab_copy(2, s).wait_recv()
        expand_into(2, lab_in[2].astype(f32).astype(jnp.int32))

    load_owners.wait()
    owned = owners_ref[...]
    b_rows = lax.broadcasted_iota(jnp.int32, (nbins, nbins), 0)
    b_cols = lax.broadcasted_iota(jnp.int32, (nbins, nbins), 1)
    column = jnp.sum(jnp.where(b_rows == b_cols, owned, 0).astype(f32), axis=1, keepdims=True)
    earlier = jnp.where((column.astype(jnp.int32) == owned) & (b_rows < b_cols), 1.0, 0.0)
    slots = jnp.sum(earlier.astype(f32), axis=0, keepdims=True)
    rows_row = (owned.astype(f32) * CAP + slots).astype(jnp.int32)
    lines = CAP * 4
    cols = 4 * nbins
    tiled = jnp.concatenate([rows_row] * 4, axis=1)
    batch = 16
    row_ids = lax.broadcasted_iota(jnp.int32, (batch * lines, cols), 0)
    col_group = lax.broadcasted_iota(jnp.int32, (batch * lines, cols), 1) // nbins
    same_line = lax.rem(row_ids, 4) == col_group
    row_slot = row_ids // 4

    def prepare(g, carry):
        chosen = same_line & (tiled == row_slot + g * (batch * CAP))
        at = pl.ds(pl.multiple_of(g * (batch * lines), 16), batch * lines)
        pick[at] = jnp.where(chosen, 1.0, 0.0).astype(bf16)
        return carry

    lax.fori_loop(0, ndev // batch, prepare, 0)

    group = min(nbins, 16)

    def pick_one(which, g, other, t, w, p, slot):
        rows = group * local
        picked = onehot[which, pl.ds(pl.multiple_of(g * rows, 16), rows), :]
        prod[slot + p] = jnp.dot(picked, other[t, 2 * w + p], preferred_element_type=f32)

    def picks(which, g, other, t, w, slot):
        for p in range(2):
            pick_one(which, g, other, t, w, p, slot)

    def add_products(sign, mine, g, t, slot):
        for b in range(group):
            rows = slice(b * local, (b + 1) * local)
            p_re, p_im = prod[slot, rows], prod[slot + 1, rows]
            o_re, o_im = mine[0], mine[1]
            re = (o_re * p_re + o_im * p_im).reshape(local // 8, 8, CHUNK)
            im = (o_im * p_re - o_re * p_im).reshape(local // 8, 8, CHUNK)
            acc[t, 0, g * group + b] += jnp.sum(re, axis=0)
            acc[t, 1, g * group + b] += jnp.sum(im, axis=0) * sign

    def take_own(t, w):
        for p in range(2):
            own[p] = white[place(par, t), 2 * w + p].astype(f32)

    sign_near = (1 - 2 * par).astype(f32)

    def part_copy(g, o, slot):
        return pltpu.make_async_remote_copy(
            src_ref=send_part.at[g, o],
            dst_ref=recv_part.at[g, slot],
            send_sem=part_send.at[g, o],
            recv_sem=part_recv.at[g, slot],
            device_id={"src": o // nrcv, "rcv": lax.rem(o, nrcv)},
            device_id_type=MESH,
        )

    def summed(t):
        rows = [
            jnp.sum(acc[t, q, :, :, d * LANES : (d + 1) * LANES], axis=1)
            for d in range(CHUNK // LANES)
            for q in range(2)
        ]
        return jnp.concatenate(rows, axis=0).astype(bf16)

    def route(g):
        stacked = [summed(2 * g + u) for u in range(2)]

        def some(q, carry):
            at = pl.ds(pl.multiple_of(q * (batch * lines), 16), batch * lines)
            wide = [jnp.dot(pick[at], rhs, preferred_element_type=f32) for rhs in stacked]
            for n in range(batch):
                both = [v[n * lines : (n + 1) * lines] for v in wide]
                send_part[g, q * batch + n] = jnp.concatenate(both, axis=0).astype(bf16)
            return carry

        lax.fori_loop(0, ndev // batch, some, 0)

        def send_one(k, carry):
            part_copy(g, lax.rem(me + k, ndev), me).start()
            return carry

        lax.fori_loop(1, ndev, send_one, 0, unroll=steps)
        recv_part[g, me] = send_part[g, me]

    acc[...] = jnp.zeros(acc.shape, f32)

    def far_piece(q):
        t, w = q // windows, lax.rem(q, windows)
        for p in range(2):
            far_copy(t, 2 * w + p).wait_recv()
        take_own(t, w)

        def some(g, carry):
            picks(1 - par, g, far, t, w, 0)
            add_products(-sign_near, own, g, t, 0)
            return carry

        lax.fori_loop(0, nbins // group, some, 0)

    def relay_piece(q, carry):
        t, w = q // windows, lax.rem(q, windows)
        for p in range(2):
            near_copy(t, 2 * w + p).wait_recv()

            @pl.when(sends_far)
            def _():
                far_copy(t, 2 * w + p).start()

        take_own(t, w)

        def some(g, carry):
            picks(par, g, near, t, w, 0)
            add_products(sign_near, own, g, t, 0)
            return carry

        lax.fori_loop(0, nbins // group, some, 0)

        return carry

    lax.fori_loop(0, relayed * windows, relay_piece, 0)

    @pl.when((par == 0) & has_far)
    def _():
        lab_copy(0, s).wait_recv()
        expand_into(1, jnp.transpose(lab_in[0].astype(f32)).astype(jnp.int32))

    @pl.when(sends_far)
    def _():
        for u in range(half - relayed):
            for k in range(parts):
                direct_copy(u, k).wait_recv()

    def direct_piece(q, carry):
        t, w = q // windows, lax.rem(q, windows)
        take_own(t, w)

        @pl.when(sends_far)
        def _():
            for p in range(2):
                own_d[p] = direct[t - relayed, 2 * w + p].astype(f32)

        for p in range(2):
            near_copy(t, 2 * w + p).wait_recv()

        def some(g, carry):
            picks(par, g, near, t, w, 0)
            picks(2, g, near, t, w, 2)
            add_products(sign_near, own, g, t, 0)
            add_products(-sign_near, own_d, g, t, 2)
            return carry

        lax.fori_loop(0, nbins // group, some, 0)

        @pl.when(has_far & (t == relayed))
        def _():
            def some_far(n, inner):
                far_piece(w * relayed + n)
                return inner

            lax.fori_loop(0, relayed, some_far, 0)

        @pl.when((t == half - 2) & (w == windows - 1))
        def _():
            route(0)

        return carry

    own_d[...] = jnp.zeros(own_d.shape, f32)
    lax.fori_loop(relayed * windows, half * windows, direct_piece, 0)

    route(1)

    def take_count(k, carry):
        o = lax.rem(s + k, nsrc)
        count_copy(o, o).wait_recv()
        return carry

    lax.fori_loop(1, nsrc, take_count, 0)
    counts = jnp.sum(count_in[...], axis=0)[0:1, :nbins]
    scale = []
    for c in range(CAP):
        mine = jnp.sum(jnp.where(rows_row == me * CAP + c, counts, 0.0), axis=1, keepdims=True)
        scale.append(1.0 / jnp.sqrt(jnp.maximum(mine, 1.0)))
    for g in range(half // 2):

        def take_part(k, carry):
            o = lax.rem(me + k, ndev)
            part_copy(g, o, o).wait_recv()
            return carry

        lax.fori_loop(1, ndev, take_part, 0, unroll=steps)
        for rr in range(nrcv):
            for pp in range(2):

                def add(z, total):
                    return total + recv_part[g, (2 * z + pp) * nrcv + rr].astype(f32)

                total = jnp.zeros((2 * lines, LANES), f32)
                total = lax.fori_loop(0, nsrc // 2, add, total, unroll=4)
                for u in range(2):
                    t = 2 * g + u
                    n = t + 1 if t < half - 2 else 0 if t == half - 2 else half - 1
                    j = pp * half + rr * (half - 1) + n * (1 - 2 * rr)
                    for c in range(CAP):
                        row = (c * nrcv * chunks + rr * chunks + j) * 4
                        value = total[u * lines + c * 4 : u * lines + c * 4 + 4]
                        out_ref[row : row + 4] = value * scale[c]

    for t in range(half):
        for k in range(parts):
            near_copy(t, k).wait_send()

    @pl.when(sends_far)
    def _():
        for t in range(relayed):
            for k in range(parts):
                far_copy(t, k).wait_send()

    @pl.when(has_far)
    def _():
        for u in range(half - relayed):
            for k in range(parts):
                direct_copy(u, k).wait_send()

    for n in range(2):
        halo_copy(n).wait_send()

    @pl.when(sends_label)
    def _():
        lab_copy(0, s + 1).wait_send()

    @pl.when(passes_label)
    def _():
        label_pass.wait_send()

    @pl.when(sends_second)
    def _():
        lab_copy(1, s - 1).wait_send()
        lab_copy(2, s + 2).wait_send()

    def end_count(k, carry):
        count_copy(lax.rem(s + k, nsrc), s).wait_send()
        return carry

    lax.fori_loop(1, nsrc, end_count, 0)

    def end_part(k, carry):
        for g in range(half // 2):
            part_copy(g, lax.rem(me + k, ndev), me).wait_send()
        return carry

    lax.fori_loop(1, ndev, end_part, 0, unroll=steps)


def per_device(spectra, pair_bins, owners):
    local, windows, _, width = spectra.shape
    nbins = owners.shape[0]
    nsrc = lax.axis_size("src")
    nrcv = lax.axis_size("rcv")
    ndev = nsrc * nrcv
    chunks = width // CHUNK
    half = chunks // 2
    relayed = half // 2
    tiles = width // LANES
    parts = 2 * windows
    lanes = -(-nbins // 128) * 128
    group = min(nbins, 16)
    x = spectra.reshape(local * windows, 2, tiles, LANES).transpose(0, 2, 1, 3)
    x = x.reshape(local * windows, 2 * tiles, LANES)
    dims = (nsrc, nrcv, nbins, local, windows, chunks)
    bf16, f32 = jnp.bfloat16, jnp.float32
    dma = pltpu.SemaphoreType.DMA
    hbm = pl.BlockSpec(memory_space=pltpu.HBM)
    args = [
        pltpu.with_memory_space_constraint(v, pltpu.HBM) for v in (x, pair_bins, owners[None])
    ]
    out = pl.pallas_call(
        functools.partial(kernel, dims),
        out_shape=jax.ShapeDtypeStruct((CAP * nrcv * tiles * 2, LANES), f32),
        in_specs=[hbm] * 3,
        out_specs=pl.BlockSpec(memory_space=pltpu.VMEM),
        scratch_shapes=[
            pltpu.VMEM((2, local * windows, tiles, LANES), bf16),
            pltpu.VMEM((windows * 2 * tiles * local, LANES), f32),
            pltpu.VMEM((chunks, parts, local, CHUNK), bf16),
            pltpu.VMEM((half, parts, local, CHUNK), bf16),
            pltpu.VMEM((relayed, parts, local, CHUNK), bf16),
            pltpu.VMEM((half - relayed, parts, local, CHUNK), bf16),
            pltpu.VMEM((windows * local, width + 2 * LANES), bf16),
            pltpu.VMEM((windows * local, width + 2 * LANES), bf16),
            pltpu.VMEM((2, windows * local, LANES), bf16),
            pltpu.VMEM((CHUNK + 2 * LANES, CHUNK), bf16),
            pltpu.VMEM((3, nbins * local, local), bf16),
            pltpu.VMEM((2, local, CHUNK), f32),
            pltpu.VMEM((2, local, CHUNK), f32),
            pltpu.VMEM((4, group * local, CHUNK), f32),
            pltpu.VMEM((half, 2, nbins, 8, CHUNK), f32),
            pltpu.VMEM((ndev * CAP * 4, 4 * nbins), bf16),
            pltpu.VMEM((half // 2, ndev, CAP * 8, LANES), bf16),
            pltpu.VMEM((half // 2, ndev, CAP * 8, LANES), bf16),
            pltpu.VMEM((local, local), jnp.int32),
            pltpu.VMEM((1, nbins), jnp.int32),
            pltpu.VMEM((local, local), bf16),
            pltpu.VMEM((3, local, local), bf16),
            pltpu.VMEM((1, lanes), f32),
            pltpu.VMEM((nsrc, 1, lanes), f32),
            dma((4,)),
            dma((half, parts)),
            dma((half, parts)),
            dma((relayed, parts)),
            dma((relayed, parts)),
            dma((half - relayed, parts)),
            dma((half - relayed, parts)),
            dma((2,)),
            dma((2,)),
            dma((3,)),
            dma((3,)),
            dma((nsrc,)),
            dma((nsrc,)),
            dma((half // 2, ndev)),
            dma((half // 2, ndev)),
        ],
        compiler_params=pltpu.CompilerParams(
            collective_id=0, has_side_effects=True, vmem_limit_bytes=48 * 1024 * 1024
        ),
    )(*args)
    out = out.reshape(CAP, nrcv * tiles, 2, LANES).transpose(0, 2, 1, 3)
    return out.reshape(CAP, 2, nrcv * width)


def solution(mesh):
    in_specs = (P(("groups", "src"), None, None, "rcv"), P(("groups", "src"), None), P("groups"))
    out_specs = P(("groups", "src", "rcv"), None, None)
    return jax.shard_map(
        per_device, mesh=mesh, in_specs=in_specs, out_specs=out_specs, check_vma=False
    )
```
